32 devices in a mesh: comp: 4 (over y, core), tile: 8 (over z, x).
Axes of the slice: x: 2, y: 2, z: 4, core: 2. Of those that a mesh axis runs over, the one named last changes fastest.
Arguments:
- column_state: float32 [4, 8, 4, 16, 2048], P('comp', 'tile'), may hold values from -6 to 6
- mixing: float32 [2, 4, 16], replicated, may hold values from 0.02 to 0.24
- vertical: float32 [2, 16, 16], replicated, may hold values from -1.5 to 1.5
- flux_coef: float32 [2, 4], replicated, may hold values from 0.5 to 1.5
- atm_block: int32 [4, 8, 16], P('comp', 'tile'), may hold values from 0 to 15
- ocean_block: int32 [4, 8, 16], P('comp', 'tile'), may hold values from 0 to 15
- tile_offset: int32 [4, 8, 16], P('comp', 'tile'), may hold values from 0 to 6
- remap_weights: bfloat16 [4, 8, 16, 128, 128], P('comp', 'tile'), may hold values from 0 to 0.119628906
- ocean_mask: int32 [8, 2048], P('tile'), may hold values 0 or 1
Outputs:
- new_state: float32 [4, 8, 4, 16, 2048], P('comp', 'tile')
The draws below stay inside these ranges and needn't reach their ends.
Inputs may be any that keep to these rules, and one draw needn't show every extreme that they name: `atm_block`: entries at comp index 3 are not read.
All inputs are finite; a program needn't handle non-finite values. No bound on the sum of `ocean_mask` on one device may be relied on, other than what follows from the above.
Results may differ from the reference program's by a relative error of at most 0.0003.
Values sent between devices are 32-bit elements; how exact they have to be, the bound alone decides.
No kernel may reach another device: no remote copies, remote signals or barrier semaphores. Data moves between devices by JAX's collectives and lax.ppermute only.
A program may use at most 64 MiB of HBM per device.

```python
import math
import jax
import jax.numpy as jnp
from jax import lax

LEV = 16
K = 4
BA = 128
BO = 128
AB = 16
REACH = 3
SUB = 2
CELLS = 2048
OB = 16
NB = 16
N_COMP = 4
N_TILE = 8


def with_ends(entries, own_key, least, high):
    spot = [jax.random.randint(jax.random.fold_in(own_key, axis), (), 0, length) for axis, length in enumerate(entries.shape)]
    longest = entries.shape.index(max(entries.shape))
    beside = spot[:longest] + [(spot[longest] + 1) % entries.shape[longest]] + spot[longest + 1:]
    return entries.at[tuple(spot)].set(least).at[tuple(beside)].set(high)


def levels(stream_key, shape, pieces, smallest, high):
    def one(position, shards_of):
        heights = jax.random.uniform(jax.random.fold_in(jax.random.fold_in(stream_key, 6), position), (shards_of,), jnp.float32, smallest / len(pieces), high / len(pieces))
        return jnp.repeat(jnp.exp(heights), shape[position] // shards_of).reshape((-1,) + (1,) * (len(shape) - position - 1))

    level = one(*pieces[0])
    for cut in pieces[1:]:
        level = level * one(*cut)
    return level


def noise(own_key, shape, deviation, bound, shards=(), kind=jnp.bfloat16):
    values = jax.random.normal(own_key, shape, jnp.float32) * deviation
    if len(shards) > 0:
        values = levels(own_key, shape, shards, -0.22, 0.18) * values
    return jnp.clip(values, min=-bound, max=bound).astype(kind)


def setup_inputs(seed: int = 0) -> dict:
    key_list = jax.random.split(jax.random.key(seed), 10)
    return {
        "column_state": noise(key_list[0], (N_COMP, N_TILE, K, LEV, CELLS), 1.0, 6.0, ((0, 4), (1, 8)), jnp.float32),
        "mixing": jnp.clip(jnp.exp(jax.random.uniform(key_list[1], (2, K, LEV), jnp.float32, math.log(0.02), math.log(0.24))), 0.02, 0.24),
        "vertical": noise(key_list[2], (2, LEV, LEV), LEV ** -0.5, 1.5, (), jnp.float32),
        "flux_coef": jnp.clip(jax.random.uniform(key_list[3], (2, K), jnp.float32, 0.5, 1.5), 0.5, 1.5),
        "atm_block": with_ends(jax.random.randint(key_list[4], (N_COMP, N_TILE, NB), 0, AB), jax.random.fold_in(key_list[4], 1), 0, AB - 1).astype(jnp.int32),
        "ocean_block": with_ends(jax.random.randint(key_list[5], (N_COMP, N_TILE, NB), 0, OB), jax.random.fold_in(key_list[5], 1), 0, OB - 1).astype(jnp.int32),
        "tile_offset": with_ends(jax.random.randint(key_list[6], (N_COMP, N_TILE, NB), 0, 2 * REACH + 1), jax.random.fold_in(key_list[6], 1), 0, 2 * REACH).astype(jnp.int32),
        "remap_weights": jnp.clip(0.119628906 * jax.random.uniform(key_list[7], (N_COMP, N_TILE, NB, BA, BO), jnp.float32) ** levels(key_list[7], (N_COMP, N_TILE, NB, BA, BO), ((0, 4), (1, 8)), -0.2, 0.2), 0.0, 0.119628906).astype(jnp.bfloat16),
        "ocean_mask": with_ends((jax.random.randint(key_list[8], (N_TILE, CELLS), 0, 4) < 3).astype(jnp.int32), jax.random.fold_in(key_list[8], 1), 0, 1),
    }


def remap_row(row):
    blocks, chosen_index, target_block, offsets, weights = row
    tiles = blocks.shape[1]
    picked = blocks[:, jnp.arange(tiles, dtype=jnp.int32)[:, None], chosen_index]
    contrib = jnp.einsum('ktnb,tnbj->tnkj', picked.astype(jnp.float32), weights.astype(jnp.float32), precision=lax.Precision.HIGHEST)
    destination = (jnp.arange(tiles, dtype=jnp.int32)[:, None] + offsets - REACH) % tiles
    empty = jnp.zeros((tiles, OB, K, BO), jnp.float32)
    return empty.at[destination, target_block].add(contrib)


def reference(column_state, mixing, vertical, flux_coef, atm_block, ocean_block, tile_offset, remap_weights, ocean_mask):
    comps = column_state.shape[0]
    tiles = column_state.shape[1]
    atmos_rows = comps - 1
    fields = jnp.moveaxis(column_state, 1, 3).reshape(comps, K, LEV, tiles * CELLS)
    is_atmos = (jnp.arange(comps, dtype=jnp.int32) < atmos_rows)
    rates = jnp.where(is_atmos[:, None, None, None], mixing[0][None, :, :, None], mixing[1][None, :, :, None])
    for sweep in range(SUB):
        laplace = jnp.roll(fields, 1, axis=3) + jnp.roll(fields, -1, axis=3) - 2.0 * fields
        fields = fields + rates * laplace
    operators = jnp.where(is_atmos[:, None, None], vertical[0][None], vertical[1][None])
    mixed = fields + jnp.einsum('clm,ckmz->cklz', operators, fields, precision=lax.Precision.HIGHEST)
    atmos_mixed = mixed[:atmos_rows]
    ocean_cycle = mixed[atmos_rows]
    surface = jnp.tanh(flux_coef[0][None, :, None] * atmos_mixed[:, :, LEV - 1] + flux_coef[1][None, :, None] * atmos_mixed[:, :, LEV - 2])
    rounded = surface.astype(jnp.bfloat16)
    blocks = rounded.reshape(atmos_rows, K, tiles, AB, BA)
    totals = lax.map(remap_row, (blocks, atm_block[:atmos_rows], ocean_block[:atmos_rows], tile_offset[:atmos_rows], remap_weights[:atmos_rows])).sum(0)
    received = totals.transpose(2, 0, 1, 3).reshape(K, tiles * CELLS)
    land = ocean_mask.reshape(tiles * CELLS).astype(jnp.float32)
    atmosphere = atmos_mixed.at[:, :, LEV - 1].add(-0.5 * surface)
    ocean = ocean_cycle.at[:, 0].add(land[None, :] * received)
    whole = jnp.concatenate([atmosphere, ocean[None]], axis=0)
    return jnp.moveaxis(whole.reshape(comps, K, LEV, tiles, CELLS), 3, 1)
```

```python
import jax
import jax.numpy as jnp
from jax import lax
from jax.sharding import PartitionSpec as P

REACH = 3
SUB = 2


def moved(value, axis, steps):
    count = lax.axis_size(axis)
    return lax.ppermute(value, axis, [(i, (i + steps) % count) for i in range(count)])


def swapped(value, axis, bit):
    count = lax.axis_size(axis)
    return lax.ppermute(value, axis, [(i, i ^ bit) for i in range(count)])


def sideways(value, steps):
    comps, tiles = lax.axis_size("comp"), lax.axis_size("tile")
    pairs = []
    for c in range(comps):
        shift = steps if c % 2 else -steps
        pairs += [(c * tiles + t, c * tiles + (t + shift) % tiles) for t in range(tiles)]
    return lax.ppermute(value, ("comp", "tile"), pairs)


def local(
    column_state,
    mixing,
    vertical,
    flux_coef,
    atm_block,
    ocean_block,
    tile_offset,
    remap_weights,
    ocean_mask,
):
    fields = column_state[0, 0]
    cells = fields.shape[2]
    across = remap_weights.shape[3]
    ocean_cells = remap_weights.shape[4]
    oblocks = cells // ocean_cells
    spread = 2 * REACH + 1
    comp_index = lax.axis_index("comp")
    comp_count = lax.axis_size("comp")
    is_atmos = comp_index < comp_count - 1
    right_core = (comp_index % 2) == 1
    group = jnp.where(is_atmos, 0, 1).astype(jnp.int32)
    rates = lax.dynamic_index_in_dim(mixing, group, 0, keepdims=False)[:, :, None]
    operator = lax.dynamic_index_in_dim(vertical, group, 0, keepdims=False)
    from_left = moved(fields[:, :, cells - SUB :], "tile", 1)
    from_right = moved(fields[:, :, :SUB], "tile", -1)
    wide = jnp.concatenate([from_left, fields, from_right], axis=2)
    for sweep in range(SUB):
        wide = wide[:, :, 1:-1] + rates * (wide[:, :, :-2] + wide[:, :, 2:] - 2.0 * wide[:, :, 1:-1])
    fields = wide
    mixed = fields + jnp.einsum("lm,kmz->klz", operator, fields, precision=lax.Precision.HIGHEST)
    surface = jnp.tanh(flux_coef[0][:, None] * mixed[:, -1] + flux_coef[1][:, None] * mixed[:, -2])
    rounded = surface.astype(jnp.bfloat16)
    blocks = rounded.reshape(rounded.shape[0], cells // across, across)
    chosen = blocks[:, atm_block[0, 0], :]
    contrib = jnp.einsum(
        "knb,nbj->nkj", chosen, remap_weights[0, 0], preferred_element_type=jnp.float32
    )
    by_offset = (tile_offset[0, 0][:, None] == jnp.arange(spread, dtype=jnp.int32)[None, :]).astype(
        jnp.float32
    )
    by_block = (ocean_block[0, 0][:, None] == jnp.arange(oblocks, dtype=jnp.int32)[None, :]).astype(
        jnp.float32
    )
    buffers = jnp.einsum(
        "nd,no,nkj->dkoj", by_offset, by_block, contrib, precision=lax.Precision.HIGHEST
    )
    buffers = buffers.reshape(spread, rounded.shape[0], cells)
    buffers = jnp.where(is_atmos, buffers, 0.0)
    left = buffers[:REACH][::-1]
    right = buffers[REACH + 1 :]
    theirs = swapped(jnp.where(right_core, left, right), "comp", 1)
    mine = jnp.where(right_core, right, left) + theirs
    received = buffers[REACH]
    for step in range(1, REACH + 1):
        received = received + sideways(mine[step - 1], step)
    bit = 1
    while bit < comp_count:
        received = received + swapped(received, "comp", bit)
        bit *= 2
    land = ocean_mask[0].astype(jnp.float32)
    atmosphere = mixed.at[:, -1].add(-0.5 * surface)
    ocean = mixed.at[:, 0].add(land[None, :] * received)
    result = jnp.where(is_atmos, atmosphere, ocean)
    return result[None, None]


def solution(mesh):
    placed = (
        P("comp", "tile", None, None, None),
        P(),
        P(),
        P(),
        P("comp", "tile", None),
        P("comp", "tile", None),
        P("comp", "tile", None),
        P("comp", "tile", None, None, None),
        P("tile", None),
    )
    return jax.shard_map(
        local,
        mesh=mesh,
        in_specs=placed,
        out_specs=P("comp", "tile", None, None, None),
        check_vma=False,
    )
```

```python
import functools

import jax
import jax.numpy as jnp
from jax import lax
from jax.experimental import pallas as pl
from jax.experimental.pallas import tpu as pltpu
from jax.sharding import PartitionSpec as P

REACH = 3
SUB = 2
LANES = 128
ROWS = 8
MID = LANES // 2
EDGES = 2 * SUB
F32 = jnp.float32
BF16 = jnp.bfloat16
VMEM = pl.BlockSpec(memory_space=pltpu.VMEM)
ANY = pl.BlockSpec(memory_space=pl.ANY)


def moved(value, axis, steps):
    count = lax.axis_size(axis)
    return lax.ppermute(value, axis, [(i, (i + steps) % count) for i in range(count)])


def swapped(value, axis, bit):
    count = lax.axis_size(axis)
    return lax.ppermute(value, axis, [(i, i ^ bit) for i in range(count)])


def sideways(value, steps):
    comps, tiles = lax.axis_size("comp"), lax.axis_size("tile")
    pairs = []
    for c in range(comps):
        shift = steps if c % 2 else -steps
        pairs += [(c * tiles + t, c * tiles + (t + shift) % tiles) for t in range(tiles)]
    return lax.ppermute(value, ("comp", "tile"), pairs)


def lanes_of(shape):
    return lax.broadcasted_iota(jnp.int32, shape, len(shape) - 1)


def turned(value, steps):
    width = value.shape[-1]
    steps = steps % width
    return value if steps == 0 else pltpu.roll(value, steps, axis=value.ndim - 1)


def atmosphere(comps):
    return lax.axis_index("comp") < comps - 1


def split(value):
    high = value.astype(BF16)
    return high, (value - high.astype(F32)).astype(BF16)


def product(vh, vl, field):
    high, low = split(field)
    dot = functools.partial(jnp.dot, preferred_element_type=F32)
    return dot(vh, high) + dot(vl, high) + dot(vh, low)


def stencil(coef, x):
    near = turned(x, 1) + turned(x, -1)
    far = turned(x, 2) + turned(x, -2)
    return coef[0] * x + coef[1] * near + coef[2] * far


def edges_kernel(comps, state, mixing, vertical, own, to_right, to_left, mix, ver, head, tail, sems):
    group = jnp.where(atmosphere(comps), 0, 1)
    cells = state.shape[-1]
    first = pltpu.make_async_copy(state.at[0, 0, :, :, pl.ds(0, LANES)], head, sems.at[0])
    last = pltpu.make_async_copy(state.at[0, 0, :, :, pl.ds(cells - LANES, LANES)], tail, sems.at[1])
    others = [
        pltpu.make_async_copy(mixing.at[group], mix, sems.at[2]),
        pltpu.make_async_copy(vertical.at[group], ver, sems.at[3]),
    ]
    for copy in [first, last] + others:
        copy.start()
    first.wait()
    last.wait()
    lane = lanes_of((ROWS, LANES))
    right = jnp.zeros((ROWS, LANES), F32)
    left = jnp.zeros((ROWS, LANES), F32)
    number = 0
    for k in range(head.shape[0]):
        for h in range(0, head.shape[1], ROWS):
            a, b = head[k, h : h + ROWS, :], tail[k, h : h + ROWS, :]
            at = SUB * number
            here = (lane >= at) & (lane < at + SUB)
            left = jnp.where(here, turned(a, at), left)
            right = jnp.where(here, turned(b, at + SUB), right)
            own[k, h : h + ROWS, :] = jnp.where(lane < MID, turned(a, SUB), turned(b, MID + 2 * SUB))
            number += 1
    to_right[...] = right
    to_left[...] = left
    for copy in others:
        copy.wait()


def interior_kernel(
    comps,
    state,
    mix,
    ver,
    weights,
    flux,
    atm,
    ocean,
    offset,
    low,
    high,
    buf,
    wide,
    coef,
    parts,
    flux_out,
    flux_s,
    atm_s,
    ocean_s,
    offset_s,
    press,
    round_ref,
    rim,
    sems,
):
    fields, levels, cells = state.shape
    blocks = cells // LANES
    copies = [
        pltpu.make_async_copy(src, dst, sems.at[i])
        for i, (src, dst) in enumerate(
            ((flux, flux_s), (atm.at[0, 0], atm_s), (ocean.at[0, 0], ocean_s), (offset.at[0, 0], offset_s))
        )
    ]
    for copy in copies:
        copy.start()
    is_atmos = atmosphere(comps)
    right_core = lax.axis_index("comp") % 2
    buf[...] = jnp.zeros_like(buf)
    wide[...] = jnp.zeros_like(wide)
    vh, vl = split(ver[...])
    parts[0] = vh
    parts[1] = vl
    square = (levels, levels)
    eye = lax.broadcasted_iota(jnp.int32, square, 0) == lanes_of(square)
    copies[0].wait()
    for k in range(fields):
        rate = jnp.sum(
            jnp.where(eye, jnp.broadcast_to(mix[k : k + 1, :], square), 0.0), axis=1, keepdims=True
        )
        far = rate * rate
        near = 2.0 * rate - 4.0 * far
        mid = 1.0 - 4.0 * rate + 6.0 * far
        for i, c in enumerate((mid, near, far)):
            coef[i, k] = jnp.broadcast_to(c, (levels, LANES))
        field = stencil((mid, near, far), state[k])
        mixed = field + product(vh, vl, field)
        low[k] = mixed[:ROWS]
        high[k] = mixed[ROWS:]
        press[k : k + 1, :] = (
            flux_s[0, k] * mixed[levels - 1 : levels, :] + flux_s[1, k] * mixed[levels - 2 : levels - 1, :]
        )
        for i in range(2):
            flux_out[i, k : k + 1, :] = jnp.full((1, LANES), flux_s[i, k], F32)
    surface = jnp.tanh(press[...])
    press[...] = jnp.where(is_atmos, surface, 0.0)
    last = high.shape[1] - 1
    for k in range(fields):
        high[k, last : last + 1, :] = high[k, last : last + 1, :] - 0.5 * press[k : k + 1, :]
    lane = lanes_of((fields, LANES))
    for b in range(blocks):
        value = press[:, b * LANES : (b + 1) * LANES].astype(BF16).astype(F32)
        if b == 0:
            value = jnp.where(lane < SUB, 0.0, value)
        if b == blocks - 1:
            value = jnp.where(lane >= LANES - SUB, 0.0, value)
        round_ref[b] = jnp.zeros(round_ref.shape[1:], F32)
        round_ref[b, :fields, :] = value
    for copy in copies[1:]:
        copy.wait()
    side = lax.broadcasted_iota(jnp.int32, (EDGES, LANES), 0) < SUB
    for n in range(weights.shape[0]):
        block = jnp.clip(atm_s[n], 0, blocks - 1)
        place = jnp.clip(ocean_s[n], 0, blocks - 1)
        distance = jnp.clip(offset_s[n], 0, 2 * REACH) - REACH
        ahead = jnp.where(distance > 0, 1, 0)
        slot = jnp.abs(distance) - 1 + jnp.where(ahead == right_core, 0, REACH)
        slot = jnp.where(distance == 0, 2 * REACH, slot)
        term = jnp.dot(round_ref[block].astype(BF16), weights[n], preferred_element_type=F32)
        buf[slot, place] = buf[slot, place] + term[:fields]
        rim[:SUB, :] = weights[n, : 2 * ROWS, :].astype(F32)[:SUB]
        rim[SUB:, :] = weights[n, LANES - 2 * ROWS :, :].astype(F32)[2 * ROWS - SUB :]
        lead = jnp.where(block == 0, 1.0, 0.0)
        trail = jnp.where(block == blocks - 1, 1.0, 0.0)
        wide[slot, place] = wide[slot, place] + jnp.where(side, lead, trail) * rim[...]


def rim_kernel(
    comps, from_left, from_right, own, coef, parts, flux, buf, wide, mine, theirs, here, edge, press
):
    fields, levels, _ = own.shape
    is_atmos = atmosphere(comps)
    lane = lanes_of((ROWS, LANES))
    number = 0
    for k in range(fields):
        for h in range(0, levels, ROWS):
            at = SUB * number
            x = own[k, h : h + ROWS, :]
            x = jnp.where(lane < SUB, turned(from_left[...], -at), x)
            beyond = (lane >= MID + 2 * SUB) & (lane < MID + 3 * SUB)
            x = jnp.where(beyond, turned(from_right[...], MID + 2 * SUB - at), x)
            c = [coef[i, k, h : h + ROWS, :] for i in range(3)]
            edge[k, h : h + ROWS, :] = stencil(c, x)
            number += 1
    for k in range(fields):
        field = edge[k]
        mixed = field + product(parts[0], parts[1], field)
        edge[k] = mixed
        press[k : k + 1, :] = (
            flux[0, k : k + 1, :] * mixed[levels - 1 : levels, :]
            + flux[1, k : k + 1, :] * mixed[levels - 2 : levels - 1, :]
        )
    surface = jnp.where(is_atmos, jnp.tanh(press[...]), 0.0)
    press[...] = surface
    for k in range(fields):
        edge[k, levels - 1 : levels, :] = edge[k, levels - 1 : levels, :] - 0.5 * press[k : k + 1, :]
    value = surface.astype(BF16).astype(F32)
    spots = [SUB + i for i in range(SUB)] + [MID + SUB + i for i in range(SUB)]
    column = [jnp.broadcast_to(value[:, s : s + 1], (fields, LANES)) for s in spots]
    for slot in range(buf.shape[0]):
        for place in range(buf.shape[1]):
            total = buf[slot, place]
            for e in range(EDGES):
                total = total + column[e] * wide[slot, place, e : e + 1, :]
            if slot < REACH:
                mine[slot, place] = total
            elif slot < 2 * REACH:
                theirs[slot - REACH, place] = total
            else:
                here[place] = total


def finish_kernel(low_in, high_in, edge, low, high, out, sems):
    fields, _, cells = low.shape
    lane = lanes_of((ROWS, LANES))
    copies = []
    for k in range(fields):
        for half, start in ((low, 0), (high, ROWS)):
            source = low_in if start == 0 else high_in
            value = edge[k, start : start + ROWS, :]
            half[k, :, :LANES] = jnp.where(lane < SUB, turned(value, -SUB), source[k, :, :LANES])
            half[k, :, cells - LANES :] = jnp.where(
                lane >= LANES - SUB, turned(value, MID - 2 * SUB), source[k, :, cells - LANES :]
            )
        copies.append(
            pltpu.make_async_copy(high.at[k], out.at[0, 0, k, pl.ds(ROWS, high.shape[1]), :], sems.at[k])
        )
        copies[-1].start()
    for copy in copies:
        copy.wait()


def ocean_kernel(comps, out_in, low_in, received, mask, out, low, sems):
    fields, rows, cells = low.shape
    is_ocean = jnp.logical_not(atmosphere(comps))
    copies = []
    for k in range(fields):
        for b in range(cells // LANES):
            at = slice(b * LANES, (b + 1) * LANES)
            land = mask[:, at].astype(F32)
            gain = jnp.where(is_ocean, land * received[b, k : k + 1, :], 0.0)
            low[k, 0:1, at] = low_in[k, 0:1, at] + gain
        copies.append(pltpu.make_async_copy(low.at[k], out.at[0, 0, k, pl.ds(0, rows), :], sems.at[k]))
        copies[-1].start()
    for copy in copies:
        copy.wait()


def call(body, out_shape, in_specs, out_specs, scratch, flops, aliases=None, name=None):
    return pl.pallas_call(
        body,
        out_shape=out_shape,
        in_specs=in_specs,
        out_specs=out_specs,
        scratch_shapes=scratch,
        input_output_aliases=aliases or {},
        compiler_params=pltpu.CompilerParams(vmem_limit_bytes=16 << 20),
        cost_estimate=pl.CostEstimate(flops=flops, bytes_accessed=flops // 8, transcendentals=0),
        name=name,
    )


def local(
    column_state,
    mixing,
    vertical,
    flux_coef,
    atm_block,
    ocean_block,
    tile_offset,
    remap_weights,
    ocean_mask,
):
    _, _, fields, levels, cells = column_state.shape
    margins, across, ocean_cells = remap_weights.shape[2:]
    blocks = cells // LANES
    spread = 2 * REACH + 1
    comps = lax.axis_size("comp")
    groups = fields * levels // ROWS
    assert across == LANES and ocean_cells == LANES and levels == 2 * ROWS
    assert groups * SUB <= LANES and cells % LANES == 0

    def f32(*shape):
        return jax.ShapeDtypeStruct(shape, F32)

    own, to_right, to_left, mix, ver = call(
        functools.partial(edges_kernel, comps),
        (f32(fields, levels, LANES), f32(ROWS, LANES), f32(ROWS, LANES), f32(fields, levels), f32(levels, levels)),
        [ANY] * 3,
        [VMEM] * 5,
        [pltpu.VMEM((fields, levels, LANES), F32)] * 2 + [pltpu.SemaphoreType.DMA((4,))],
        10**5,
        name="edges",
    )(column_state, mixing, vertical)
    from_left = moved(to_right, "tile", 1)
    from_right = moved(to_left, "tile", -1)
    low, high, buf, wide, coef, parts, flux = call(
        functools.partial(interior_kernel, comps),
        (
            f32(fields, ROWS, cells),
            f32(fields, levels - ROWS, cells),
            f32(spread, blocks, fields, LANES),
            f32(spread, blocks, EDGES, LANES),
            f32(3, fields, levels, LANES),
            jax.ShapeDtypeStruct((2, levels, levels), BF16),
            f32(2, fields, LANES),
        ),
        [VMEM] * 4 + [ANY] * 4,
        [VMEM] * 7,
        [
            pltpu.SMEM(flux_coef.shape, F32),
            pltpu.SMEM((margins,), jnp.int32),
            pltpu.SMEM((margins,), jnp.int32),
            pltpu.SMEM((margins,), jnp.int32),
            pltpu.VMEM((fields, cells), F32),
            pltpu.VMEM((blocks, ROWS, LANES), F32),
            pltpu.VMEM((EDGES, LANES), F32),
            pltpu.SemaphoreType.DMA((4,)),
        ],
        10**7,
        name="interior",
    )(column_state[0, 0], mix, ver, remap_weights[0, 0], flux_coef, atm_block, ocean_block, tile_offset)
    mine, theirs, received, edge = call(
        functools.partial(rim_kernel, comps),
        (
            f32(REACH, blocks, fields, LANES),
            f32(REACH, blocks, fields, LANES),
            f32(blocks, fields, LANES),
            f32(fields, levels, LANES),
        ),
        [VMEM] * 8,
        [VMEM] * 4,
        [pltpu.VMEM((fields, LANES), F32)],
        10**6,
        name="rim",
    )(from_left, from_right, own, coef, parts, flux, buf, wide)
    mine = mine + swapped(theirs, "comp", 1)
    for step in range(1, REACH + 1):
        received = received + sideways(mine[step - 1], step)
    low, high, out = call(
        finish_kernel,
        (
            f32(fields, ROWS, cells),
            f32(fields, levels - ROWS, cells),
            jax.ShapeDtypeStruct(column_state.shape, F32),
        ),
        [VMEM] * 3,
        [VMEM, VMEM, ANY],
        [pltpu.SemaphoreType.DMA((fields,))],
        10**7,
        aliases={0: 0, 1: 1},
        name="finish",
    )(low, high, edge)
    bit = 1
    while bit < comps:
        received = received + swapped(received, "comp", bit)
        bit *= 2
    out, _ = call(
        functools.partial(ocean_kernel, comps),
        (jax.ShapeDtypeStruct(column_state.shape, F32), f32(fields, ROWS, cells)),
        [ANY, VMEM, VMEM, VMEM],
        [ANY, VMEM],
        [pltpu.SemaphoreType.DMA((fields,))],
        10**6,
        aliases={0: 0, 1: 1},
        name="ocean",
    )(out, low, received, ocean_mask)
    return out


def solution(mesh):
    placed = (
        P("comp", "tile", None, None, None),
        P(),
        P(),
        P(),
        P("comp", "tile", None),
        P("comp", "tile", None),
        P("comp", "tile", None),
        P("comp", "tile", None, None, None),
        P("tile", None),
    )
    return jax.shard_map(
        local,
        mesh=mesh,
        in_specs=placed,
        out_specs=P("comp", "tile", None, None, None),
        check_vma=False,
    )
```

```python
import functools

import jax
import jax.numpy as jnp
from jax import lax
from jax.experimental import pallas as pl
from jax.experimental.pallas import tpu as pltpu
from jax.sharding import PartitionSpec as P

REACH = 3
SUB = 2
LANES = 128
ROWS = 8
MID = LANES // 2
EDGES = 2 * SUB
F32 = jnp.float32
BF16 = jnp.bfloat16
VMEM = pl.BlockSpec(memory_space=pltpu.VMEM)
HBM = pl.BlockSpec(memory_space=pltpu.HBM)


def moved(value, axis, steps):
    count = lax.axis_size(axis)
    return lax.ppermute(value, axis, [(i, (i + steps) % count) for i in range(count)])


def swapped(value, axis, bit):
    count = lax.axis_size(axis)
    return lax.ppermute(value, axis, [(i, i ^ bit) for i in range(count)])


def sideways(value, steps):
    comps, tiles = lax.axis_size("comp"), lax.axis_size("tile")
    pairs = []
    for c in range(comps):
        shift = steps if c % 2 else -steps
        pairs += [(c * tiles + t, c * tiles + (t + shift) % tiles) for t in range(tiles)]
    return lax.ppermute(value, ("comp", "tile"), pairs)


def in_hbm(*arrays):
    return [pltpu.with_memory_space_constraint(a, pltpu.HBM) for a in arrays]


def lanes_of(shape):
    return lax.broadcasted_iota(jnp.int32, shape, len(shape) - 1)


def turned(value, steps):
    width = value.shape[-1]
    steps = steps % width
    return value if steps == 0 else pltpu.roll(value, steps, axis=value.ndim - 1)


def atmosphere(comps):
    return lax.axis_index("comp") < comps - 1


def split(value):
    high = value.astype(BF16)
    return high, (value - high.astype(F32)).astype(BF16)


def product(vh, vl, field):
    high, low = split(field)
    dot = functools.partial(jnp.dot, preferred_element_type=F32)
    return dot(vh, high) + dot(vl, high) + dot(vh, low)


def stencil(coef, x):
    near = turned(x, 1) + turned(x, -1)
    far = turned(x, 2) + turned(x, -2)
    return coef[0] * x + coef[1] * near + coef[2] * far


def edges_kernel(comps, state, mixing, vertical, own, to_right, to_left, mix, ver, head, tail, sems):
    group = jnp.where(atmosphere(comps), 0, 1)
    cells = state.shape[-1]
    first = pltpu.make_async_copy(state.at[0, 0, :, :, pl.ds(0, LANES)], head, sems.at[0])
    last = pltpu.make_async_copy(state.at[0, 0, :, :, pl.ds(cells - LANES, LANES)], tail, sems.at[1])
    others = [
        pltpu.make_async_copy(mixing.at[group], mix, sems.at[2]),
        pltpu.make_async_copy(vertical.at[group], ver, sems.at[3]),
    ]
    for copy in [first, last] + others:
        copy.start()
    first.wait()
    last.wait()
    lane = lanes_of((ROWS, LANES))
    right = jnp.zeros((ROWS, LANES), F32)
    left = jnp.zeros((ROWS, LANES), F32)
    number = 0
    for k in range(head.shape[0]):
        for h in range(0, head.shape[1], ROWS):
            a, b = head[k, h : h + ROWS, :], tail[k, h : h + ROWS, :]
            at = SUB * number
            here = (lane >= at) & (lane < at + SUB)
            left = jnp.where(here, turned(a, at), left)
            right = jnp.where(here, turned(b, at + SUB), right)
            own[k, h : h + ROWS, :] = jnp.where(lane < MID, turned(a, SUB), turned(b, MID + 2 * SUB))
            number += 1
    to_right[...] = right
    to_left[...] = left
    for copy in others:
        copy.wait()


def interior_kernel(
    comps,
    state,
    mix,
    ver,
    weights_hbm,
    flux,
    atm,
    ocean,
    offset,
    low,
    high,
    buf,
    wide,
    coef,
    parts,
    flux_out,
    flux_s,
    atm_s,
    ocean_s,
    offset_s,
    press,
    round_ref,
    rim,
    weights,
    sems,
):
    fields, levels, cells = state.shape
    blocks = cells // LANES
    copies = [
        pltpu.make_async_copy(src, dst, sems.at[i])
        for i, (src, dst) in enumerate(
            (
                (flux, flux_s),
                (atm.at[0, 0], atm_s),
                (ocean.at[0, 0], ocean_s),
                (offset.at[0, 0], offset_s),
                (weights_hbm.at[0, 0], weights),
            )
        )
    ]
    for copy in copies:
        copy.start()
    is_atmos = atmosphere(comps)
    right_core = lax.axis_index("comp") % 2
    buf[...] = jnp.zeros_like(buf)
    wide[...] = jnp.zeros_like(wide)
    vh, vl = split(ver[...])
    parts[0] = vh
    parts[1] = vl
    square = (levels, levels)
    eye = lax.broadcasted_iota(jnp.int32, square, 0) == lanes_of(square)
    copies[0].wait()
    for k in range(fields):
        rate = jnp.sum(
            jnp.where(eye, jnp.broadcast_to(mix[k : k + 1, :], square), 0.0), axis=1, keepdims=True
        )
        far = rate * rate
        near = 2.0 * rate - 4.0 * far
        mid = 1.0 - 4.0 * rate + 6.0 * far
        for i, c in enumerate((mid, near, far)):
            coef[i, k] = jnp.broadcast_to(c, (levels, LANES))
        field = stencil((mid, near, far), state[k])
        mixed = field + product(vh, vl, field)
        low[k] = mixed[:ROWS]
        high[k] = mixed[ROWS:]
        press[k : k + 1, :] = (
            flux_s[0, k] * mixed[levels - 1 : levels, :] + flux_s[1, k] * mixed[levels - 2 : levels - 1, :]
        )
        for i in range(2):
            flux_out[i, k : k + 1, :] = jnp.full((1, LANES), flux_s[i, k], F32)
    surface = jnp.tanh(press[...])
    press[...] = jnp.where(is_atmos, surface, 0.0)
    last = high.shape[1] - 1
    for k in range(fields):
        high[k, last : last + 1, :] = high[k, last : last + 1, :] - 0.5 * press[k : k + 1, :]
    lane = lanes_of((fields, LANES))
    for b in range(blocks):
        value = press[:, b * LANES : (b + 1) * LANES].astype(BF16).astype(F32)
        if b == 0:
            value = jnp.where(lane < SUB, 0.0, value)
        if b == blocks - 1:
            value = jnp.where(lane >= LANES - SUB, 0.0, value)
        round_ref[b] = jnp.zeros(round_ref.shape[1:], F32)
        round_ref[b, :fields, :] = value
    for copy in copies[1:]:
        copy.wait()
    side = lax.broadcasted_iota(jnp.int32, (EDGES, LANES), 0) < SUB
    for n in range(weights.shape[0]):
        block = jnp.clip(atm_s[n], 0, blocks - 1)
        place = jnp.clip(ocean_s[n], 0, blocks - 1)
        distance = jnp.clip(offset_s[n], 0, 2 * REACH) - REACH
        ahead = jnp.where(distance > 0, 1, 0)
        slot = jnp.abs(distance) - 1 + jnp.where(ahead == right_core, 0, REACH)
        slot = jnp.where(distance == 0, 2 * REACH, slot)
        term = jnp.dot(round_ref[block].astype(BF16), weights[n], preferred_element_type=F32)
        buf[slot, place] = buf[slot, place] + term[:fields]
        rim[:SUB, :] = weights[n, : 2 * ROWS, :].astype(F32)[:SUB]
        rim[SUB:, :] = weights[n, LANES - 2 * ROWS :, :].astype(F32)[2 * ROWS - SUB :]
        lead = jnp.where(block == 0, 1.0, 0.0)
        trail = jnp.where(block == blocks - 1, 1.0, 0.0)
        wide[slot, place] = wide[slot, place] + jnp.where(side, lead, trail) * rim[...]


def rim_kernel(
    comps, from_left, from_right, own, coef, parts, flux, buf, wide, mine, theirs, here, edge, press
):
    fields, levels, _ = own.shape
    is_atmos = atmosphere(comps)
    lane = lanes_of((ROWS, LANES))
    number = 0
    for k in range(fields):
        for h in range(0, levels, ROWS):
            at = SUB * number
            x = own[k, h : h + ROWS, :]
            x = jnp.where(lane < SUB, turned(from_left[...], -at), x)
            beyond = (lane >= MID + 2 * SUB) & (lane < MID + 3 * SUB)
            x = jnp.where(beyond, turned(from_right[...], MID + 2 * SUB - at), x)
            c = [coef[i, k, h : h + ROWS, :] for i in range(3)]
            edge[k, h : h + ROWS, :] = stencil(c, x)
            number += 1
    for k in range(fields):
        field = edge[k]
        mixed = field + product(parts[0], parts[1], field)
        edge[k] = mixed
        press[k : k + 1, :] = (
            flux[0, k : k + 1, :] * mixed[levels - 1 : levels, :]
            + flux[1, k : k + 1, :] * mixed[levels - 2 : levels - 1, :]
        )
    surface = jnp.where(is_atmos, jnp.tanh(press[...]), 0.0)
    press[...] = surface
    for k in range(fields):
        edge[k, levels - 1 : levels, :] = edge[k, levels - 1 : levels, :] - 0.5 * press[k : k + 1, :]
    value = surface.astype(BF16).astype(F32)
    spots = [SUB + i for i in range(SUB)] + [MID + SUB + i for i in range(SUB)]
    column = [jnp.broadcast_to(value[:, s : s + 1], (fields, LANES)) for s in spots]
    for slot in range(buf.shape[0]):
        for place in range(buf.shape[1]):
            total = buf[slot, place]
            for e in range(EDGES):
                total = total + column[e] * wide[slot, place, e : e + 1, :]
            if slot < REACH:
                mine[slot, place] = total
            elif slot < 2 * REACH:
                theirs[slot - REACH, place] = total
            else:
                here[place] = total


def finish_kernel(comps, low_in, high_in, edge, mask, low, high, land, out, raw, sems):
    fields, _, cells = low.shape
    lane = lanes_of((ROWS, LANES))
    copies = [pltpu.make_async_copy(mask, raw, sems.at[fields])]
    copies[0].start()
    for k in range(fields):
        for half, start in ((low, 0), (high, ROWS)):
            source = low_in if start == 0 else high_in
            value = edge[k, start : start + ROWS, :]
            half[k, :, :LANES] = jnp.where(lane < SUB, turned(value, -SUB), source[k, :, :LANES])
            half[k, :, cells - LANES :] = jnp.where(
                lane >= LANES - SUB, turned(value, MID - 2 * SUB), source[k, :, cells - LANES :]
            )
        copies.append(
            pltpu.make_async_copy(high.at[k], out.at[0, 0, k, pl.ds(ROWS, high.shape[1]), :], sems.at[k])
        )
        copies[-1].start()
    for copy in copies:
        copy.wait()
    land[...] = jnp.where(atmosphere(comps), 0.0, raw[...].astype(F32))


def ocean_kernel(out_in, low_in, received, land, out, low, sems):
    fields, rows, cells = low.shape
    copies = []
    for k in range(fields):
        for b in range(cells // LANES):
            at = slice(b * LANES, (b + 1) * LANES)
            low[k, 0:1, at] = low_in[k, 0:1, at] + land[:, at] * received[b, k : k + 1, :]
        copies.append(pltpu.make_async_copy(low.at[k], out.at[0, 0, k, pl.ds(0, rows), :], sems.at[k]))
        copies[-1].start()
    for copy in copies:
        copy.wait()


def call(body, out_shape, in_specs, out_specs, scratch, flops, aliases=None):
    return pl.pallas_call(
        body,
        out_shape=out_shape,
        in_specs=in_specs,
        out_specs=out_specs,
        scratch_shapes=scratch,
        input_output_aliases=aliases or {},
        compiler_params=pltpu.CompilerParams(vmem_limit_bytes=16 << 20),
        cost_estimate=pl.CostEstimate(flops=flops, bytes_accessed=flops // 8, transcendentals=0),
    )


def step(
    column_state,
    mixing,
    vertical,
    flux_coef,
    atm_block,
    ocean_block,
    tile_offset,
    remap_weights,
    ocean_mask,
):
    _, _, fields, levels, cells = column_state.shape
    margins, across, ocean_cells = remap_weights.shape[2:]
    blocks = cells // LANES
    spread = 2 * REACH + 1
    comps = lax.axis_size("comp")
    groups = fields * levels // ROWS
    assert across == LANES and ocean_cells == LANES and levels == 2 * ROWS
    assert groups * SUB <= LANES and cells % LANES == 0

    def f32(*shape):
        return jax.ShapeDtypeStruct(shape, F32)

    own, to_right, to_left, mix, ver = call(
        functools.partial(edges_kernel, comps),
        (f32(fields, levels, LANES), f32(ROWS, LANES), f32(ROWS, LANES), f32(fields, levels), f32(levels, levels)),
        [HBM] * 3,
        [VMEM] * 5,
        [pltpu.VMEM((fields, levels, LANES), F32)] * 2 + [pltpu.SemaphoreType.DMA((4,))],
        10**5,
    )(*in_hbm(column_state, mixing, vertical))
    from_left = moved(to_right, "tile", 1)
    from_right = moved(to_left, "tile", -1)
    low, high, buf, wide, coef, parts, flux = call(
        functools.partial(interior_kernel, comps),
        (
            f32(fields, ROWS, cells),
            f32(fields, levels - ROWS, cells),
            f32(spread, blocks, fields, LANES),
            f32(spread, blocks, EDGES, LANES),
            f32(3, fields, levels, LANES),
            jax.ShapeDtypeStruct((2, levels, levels), BF16),
            f32(2, fields, LANES),
        ),
        [VMEM] * 3 + [HBM] * 5,
        [VMEM] * 7,
        [
            pltpu.SMEM(flux_coef.shape, F32),
            pltpu.SMEM((margins,), jnp.int32),
            pltpu.SMEM((margins,), jnp.int32),
            pltpu.SMEM((margins,), jnp.int32),
            pltpu.VMEM((fields, cells), F32),
            pltpu.VMEM((blocks, ROWS, LANES), F32),
            pltpu.VMEM((EDGES, LANES), F32),
            pltpu.VMEM(remap_weights.shape[2:], BF16),
            pltpu.SemaphoreType.DMA((5,)),
        ],
        10**7,
    )(column_state[0, 0], mix, ver, *in_hbm(remap_weights, flux_coef, atm_block, ocean_block, tile_offset))
    mine, theirs, received, edge = call(
        functools.partial(rim_kernel, comps),
        (
            f32(REACH, blocks, fields, LANES),
            f32(REACH, blocks, fields, LANES),
            f32(blocks, fields, LANES),
            f32(fields, levels, LANES),
        ),
        [VMEM] * 8,
        [VMEM] * 4,
        [pltpu.VMEM((fields, LANES), F32)],
        10**6,
    )(from_left, from_right, own, coef, parts, flux, buf, wide)
    mine = mine + swapped(theirs, "comp", 1)
    for step in range(REACH, 0, -1):
        arrived = sideways(mine[step - 1], step)
        received = received + arrived
    low, high, land, out = call(
        functools.partial(finish_kernel, comps),
        (
            f32(fields, ROWS, cells),
            f32(fields, levels - ROWS, cells),
            f32(1, cells),
            jax.ShapeDtypeStruct(column_state.shape, F32),
        ),
        [VMEM] * 3 + [HBM],
        [VMEM, VMEM, VMEM, HBM],
        [pltpu.VMEM(ocean_mask.shape, jnp.int32), pltpu.SemaphoreType.DMA((fields + 1,))],
        10**7,
        aliases={0: 0, 1: 1},
    )(low, high, edge, *in_hbm(ocean_mask))
    bit = 1
    while bit < comps:
        received = received + swapped(received, "comp", bit)
        bit *= 2
    out, _ = call(
        ocean_kernel,
        (jax.ShapeDtypeStruct(column_state.shape, F32), f32(fields, ROWS, cells)),
        [HBM, VMEM, VMEM, VMEM],
        [HBM, VMEM],
        [pltpu.SemaphoreType.DMA((fields,))],
        10**6,
        aliases={0: 0, 1: 1},
    )(out, low, received, land)
    return out


def solution(mesh):
    placed = (
        P("comp", "tile", None, None, None),
        P(),
        P(),
        P(),
        P("comp", "tile", None),
        P("comp", "tile", None),
        P("comp", "tile", None),
        P("comp", "tile", None, None, None),
        P("tile", None),
    )
    return jax.shard_map(
        step,
        mesh=mesh,
        in_specs=placed,
        out_specs=P("comp", "tile", None, None, None),
        check_vma=False,
    )
```

```python
import functools

import jax
import jax.numpy as jnp
from jax import lax
from jax.experimental import pallas as pl
from jax.experimental.pallas import tpu as pltpu
from jax.sharding import PartitionSpec as P

REACH = 3
SUB = 2
LANES = 128
ROWS = 8
MID = LANES // 2
EDGES = 2 * SUB
F32 = jnp.float32
BF16 = jnp.bfloat16
VMEM = pl.BlockSpec(memory_space=pltpu.VMEM)
HBM = pl.BlockSpec(memory_space=pltpu.HBM)


def moved(value, axis, steps):
    count = lax.axis_size(axis)
    return lax.ppermute(value, axis, [(i, (i + steps) % count) for i in range(count)])


def gathered(value):
    comps = lax.axis_size("comp")
    last = comps - 1
    if comps == 4:
        cycles = [(1, last, 2, 0), (0, last, 2, 1)]
        paths = [list(zip(c, c[1:] + c[:1])) for c in cycles]
        paths.append([(i, i ^ 1) for i in range(comps)])
    else:
        paths = [[(i, (i + s) % comps) for i in range(comps)] for s in range(1, comps)]
    total = value
    for pairs in paths:
        arrived = lax.ppermute(value, "comp", pairs)
        total = total + arrived
    return total


def swapped(value, axis, bit):
    count = lax.axis_size(axis)
    return lax.ppermute(value, axis, [(i, i ^ bit) for i in range(count)])


def sideways(value, steps):
    comps, tiles = lax.axis_size("comp"), lax.axis_size("tile")
    pairs = []
    for c in range(comps):
        shift = steps if c % 2 else -steps
        pairs += [(c * tiles + t, c * tiles + (t + shift) % tiles) for t in range(tiles)]
    return lax.ppermute(value, ("comp", "tile"), pairs)


def in_hbm(*arrays):
    return [pltpu.with_memory_space_constraint(a, pltpu.HBM) for a in arrays]


def lanes_of(shape):
    return lax.broadcasted_iota(jnp.int32, shape, len(shape) - 1)


def turned(value, steps):
    width = value.shape[-1]
    steps = steps % width
    return value if steps == 0 else pltpu.roll(value, steps, axis=value.ndim - 1)


def atmosphere(comps):
    return lax.axis_index("comp") < comps - 1


def split(value):
    high = value.astype(BF16)
    return high, (value - high.astype(F32)).astype(BF16)


def product(vh, vl, field):
    high, low = split(field)
    dot = functools.partial(jnp.dot, preferred_element_type=F32)
    return dot(vh, high) + dot(vl, high) + dot(vh, low)


def stencil(coef, x):
    near = turned(x, 1) + turned(x, -1)
    far = turned(x, 2) + turned(x, -2)
    return coef[0] * x + coef[1] * near + coef[2] * far


def edges_kernel(comps, state, mixing, vertical, own, to_right, to_left, mix, ver, head, tail, sems):
    group = jnp.where(atmosphere(comps), 0, 1)
    cells = state.shape[-1]
    first = pltpu.make_async_copy(state.at[0, 0, :, :, pl.ds(0, LANES)], head, sems.at[0])
    last = pltpu.make_async_copy(state.at[0, 0, :, :, pl.ds(cells - LANES, LANES)], tail, sems.at[1])
    others = [
        pltpu.make_async_copy(mixing.at[group], mix, sems.at[2]),
        pltpu.make_async_copy(vertical.at[group], ver, sems.at[3]),
    ]
    for copy in [first, last] + others:
        copy.start()
    first.wait()
    last.wait()
    lane = lanes_of((ROWS, LANES))
    right = jnp.zeros((ROWS, LANES), F32)
    left = jnp.zeros((ROWS, LANES), F32)
    number = 0
    for k in range(head.shape[0]):
        for h in range(0, head.shape[1], ROWS):
            a, b = head[k, h : h + ROWS, :], tail[k, h : h + ROWS, :]
            at = SUB * number
            here = (lane >= at) & (lane < at + SUB)
            left = jnp.where(here, turned(a, at), left)
            right = jnp.where(here, turned(b, at + SUB), right)
            own[k, h : h + ROWS, :] = jnp.where(lane < MID, turned(a, SUB), turned(b, MID + 2 * SUB))
            number += 1
    to_right[...] = right
    to_left[...] = left
    for copy in others:
        copy.wait()


def column_of(row, square):
    eye = lax.broadcasted_iota(jnp.int32, square, 0) == lanes_of(square)
    return jnp.sum(jnp.where(eye, jnp.broadcast_to(row, square), 0.0), axis=1, keepdims=True)


def interior_kernel(
    comps,
    state,
    mix,
    ver,
    weights_hbm,
    flux,
    atm,
    ocean,
    offset,
    spread_out,
    buf,
    wide,
    coef,
    lean,
    flux_s,
    atm_s,
    ocean_s,
    offset_s,
    press,
    round_ref,
    rim,
    weights,
    sems,
):
    fields, levels, cells = state.shape
    blocks = cells // LANES
    copies = [
        pltpu.make_async_copy(src, dst, sems.at[i])
        for i, (src, dst) in enumerate(
            (
                (flux, flux_s),
                (atm.at[0, 0], atm_s),
                (ocean.at[0, 0], ocean_s),
                (offset.at[0, 0], offset_s),
                (weights_hbm.at[0, 0], weights),
            )
        )
    ]
    for copy in copies:
        copy.start()
    is_atmos = atmosphere(comps)
    right_core = lax.axis_index("comp") % 2
    buf[...] = jnp.zeros_like(buf)
    wide[...] = jnp.zeros_like(wide)
    square = (levels, levels)
    lane = lanes_of((1, levels))
    last = ver[levels - 1 : levels, :] + jnp.where(lane == levels - 1, 1.0, 0.0)
    second = ver[levels - 2 : levels - 1, :] + jnp.where(lane == levels - 2, 1.0, 0.0)
    last, second = column_of(last, square), column_of(second, square)
    for k in range(fields):
        rate = column_of(mix[k : k + 1, :], square)
        far = rate * rate
        near = 2.0 * rate - 4.0 * far
        mid = 1.0 - 4.0 * rate + 6.0 * far
        for i, c in enumerate((mid, near, far)):
            coef[i, k] = jnp.broadcast_to(c, (levels, LANES))
        spread_out[k] = stencil((mid, near, far), state[k])
    copies[0].wait()
    for k in range(fields):
        pull = flux_s[0, k] * last + flux_s[1, k] * second
        lean[k] = jnp.broadcast_to(pull, (levels, LANES))
        press[k : k + 1, :] = jnp.sum(pull * spread_out[k], axis=0, keepdims=True)
    surface = jnp.where(is_atmos, jnp.tanh(press[...]), 0.0).astype(BF16).astype(F32)
    lane = lanes_of((fields, LANES))
    round_ref[...] = jnp.zeros_like(round_ref)
    for b in range(blocks):
        value = surface[:, b * LANES : (b + 1) * LANES]
        if b == 0:
            value = jnp.where(lane < SUB, 0.0, value)
        if b == blocks - 1:
            value = jnp.where(lane >= LANES - SUB, 0.0, value)
        round_ref[b, :fields, :] = value
    for copy in copies[1:]:
        copy.wait()
    side = lax.broadcasted_iota(jnp.int32, (EDGES, LANES), 0) < SUB
    for n in range(weights.shape[0]):
        block = jnp.clip(atm_s[n], 0, blocks - 1)
        place = jnp.clip(ocean_s[n], 0, blocks - 1)
        distance = jnp.clip(offset_s[n], 0, 2 * REACH) - REACH
        ahead = jnp.where(distance > 0, 1, 0)
        slot = jnp.abs(distance) - 1 + jnp.where(ahead == right_core, 0, REACH)
        slot = jnp.where(distance == 0, 2 * REACH, slot)
        term = jnp.dot(round_ref[block].astype(BF16), weights[n], preferred_element_type=F32)
        buf[slot, place] = buf[slot, place] + term[:fields]
        rim[n, :SUB, :] = weights[n, : 2 * ROWS, :].astype(F32)[:SUB]
        rim[n, SUB:, :] = weights[n, LANES - 2 * ROWS :, :].astype(F32)[2 * ROWS - SUB :]
        lead = jnp.where(block == 0, 1.0, 0.0)
        trail = jnp.where(block == blocks - 1, 1.0, 0.0)
        wide[slot, place] = wide[slot, place] + jnp.where(side, lead, trail) * rim[n]


def rim_kernel(
    comps, from_left, from_right, own, coef, lean, buf, wide, mine, theirs, here, edge, press
):
    fields, levels, _ = own.shape
    lane = lanes_of((ROWS, LANES))
    beyond = (lane >= MID + 2 * SUB) & (lane < MID + 3 * SUB)
    number = 0
    for k in range(fields):
        total = jnp.zeros((ROWS, LANES), F32)
        for h in range(0, levels, ROWS):
            at = SUB * number
            x = own[k, h : h + ROWS, :]
            x = jnp.where(lane < SUB, turned(from_left[...], -at), x)
            x = jnp.where(beyond, turned(from_right[...], MID + 2 * SUB - at), x)
            field = stencil([coef[i, k, h : h + ROWS, :] for i in range(3)], x)
            edge[k, h : h + ROWS, :] = field
            total = total + lean[k, h : h + ROWS, :] * field
            number += 1
        press[k : k + 1, :] = jnp.sum(total, axis=0, keepdims=True)
    value = jnp.where(atmosphere(comps), jnp.tanh(press[...]), 0.0).astype(BF16).astype(F32)
    spots = [SUB + i for i in range(SUB)] + [MID + SUB + i for i in range(SUB)]
    column = [jnp.broadcast_to(value[:, s : s + 1], (fields, LANES)) for s in spots]
    for slot in range(buf.shape[0]):
        for place in range(buf.shape[1]):
            total = buf[slot, place]
            for e in range(EDGES):
                total = total + column[e] * wide[slot, place, e : e + 1, :]
            if slot < REACH:
                mine[slot, place] = total
            elif slot < 2 * REACH:
                theirs[slot - REACH, place] = total
            else:
                here[place] = total


def finish_kernel(comps, field_in, edge, ver, flux, mask, low, land, out, high, press, raw, flux_s, sems):
    fields, levels, cells = field_in.shape
    copies = [
        pltpu.make_async_copy(mask, raw, sems.at[2 * fields]),
        pltpu.make_async_copy(flux, flux_s, sems.at[2 * fields + 1]),
    ]
    for copy in copies:
        copy.start()
    vh, vl = split(ver[...])
    lane = lanes_of((levels, LANES))
    is_atmos = atmosphere(comps)
    copies[1].wait()
    waits = [copies[0]]
    for k in range(fields):
        value = edge[k]
        first = jnp.where(lane < SUB, turned(value, -SUB), field_in[k, :, :LANES])
        last = jnp.where(lane >= LANES - SUB, turned(value, MID - 2 * SUB), field_in[k, :, cells - LANES :])
        field = jnp.concatenate([first, field_in[k, :, LANES : cells - LANES], last], axis=1)
        mixed = field + product(vh, vl, field)
        low[k] = mixed[:ROWS]
        high[k] = mixed[ROWS:]
        press[k : k + 1, :] = (
            flux_s[0, k] * mixed[levels - 1 : levels, :] + flux_s[1, k] * mixed[levels - 2 : levels - 1, :]
        )
        waits.append(pltpu.make_async_copy(low.at[k], out.at[0, 0, k, pl.ds(0, ROWS), :], sems.at[k]))
        waits[-1].start()
    press[...] = jnp.where(is_atmos, jnp.tanh(press[...]), 0.0)
    end = high.shape[1] - 1
    for k in range(fields):
        high[k, end : end + 1, :] = high[k, end : end + 1, :] - 0.5 * press[k : k + 1, :]
        waits.append(
            pltpu.make_async_copy(
                high.at[k], out.at[0, 0, k, pl.ds(ROWS, levels - ROWS), :], sems.at[fields + k]
            )
        )
        waits[-1].start()
    for copy in waits:
        copy.wait()
    land[...] = raw[...].astype(F32)


def ocean_kernel(comps, out_in, low_in, received, land, out, low, sems):
    fields, rows, cells = low.shape

    @pl.when(jnp.logical_not(atmosphere(comps)))
    def _():
        copies = []
        for k in range(fields):
            for b in range(cells // LANES):
                at = slice(b * LANES, (b + 1) * LANES)
                low[k, 0:1, at] = low_in[k, 0:1, at] + land[:, at] * received[b, k : k + 1, :]
            copies.append(
                pltpu.make_async_copy(low.at[k], out.at[0, 0, k, pl.ds(0, rows), :], sems.at[k])
            )
            copies[-1].start()
        for copy in copies:
            copy.wait()


def call(body, out_shape, in_specs, out_specs, scratch, flops, aliases=None):
    return pl.pallas_call(
        body,
        out_shape=out_shape,
        in_specs=in_specs,
        out_specs=out_specs,
        scratch_shapes=scratch,
        input_output_aliases=aliases or {},
        compiler_params=pltpu.CompilerParams(vmem_limit_bytes=16 << 20),
        cost_estimate=pl.CostEstimate(flops=flops, bytes_accessed=flops // 8, transcendentals=0),
    )


def step(
    column_state,
    mixing,
    vertical,
    flux_coef,
    atm_block,
    ocean_block,
    tile_offset,
    remap_weights,
    ocean_mask,
):
    _, _, fields, levels, cells = column_state.shape
    margins, across, ocean_cells = remap_weights.shape[2:]
    blocks = cells // LANES
    spread = 2 * REACH + 1
    comps = lax.axis_size("comp")
    groups = fields * levels // ROWS
    assert across == LANES and ocean_cells == LANES and levels == 2 * ROWS
    assert groups * SUB <= LANES and cells % LANES == 0

    def f32(*shape):
        return jax.ShapeDtypeStruct(shape, F32)

    own, to_right, to_left, mix, ver = call(
        functools.partial(edges_kernel, comps),
        (f32(fields, levels, LANES), f32(ROWS, LANES), f32(ROWS, LANES), f32(fields, levels), f32(levels, levels)),
        [HBM] * 3,
        [VMEM] * 5,
        [pltpu.VMEM((fields, levels, LANES), F32)] * 2 + [pltpu.SemaphoreType.DMA((4,))],
        10**5,
    )(*in_hbm(column_state, mixing, vertical))
    from_left = moved(to_right, "tile", 1)
    from_right = moved(to_left, "tile", -1)
    field, buf, wide, coef, lean = call(
        functools.partial(interior_kernel, comps),
        (
            f32(fields, levels, cells),
            f32(spread, blocks, fields, LANES),
            f32(spread, blocks, EDGES, LANES),
            f32(3, fields, levels, LANES),
            f32(fields, levels, LANES),
        ),
        [VMEM] * 3 + [HBM] * 5,
        [VMEM] * 5,
        [
            pltpu.SMEM(flux_coef.shape, F32),
            pltpu.SMEM((margins,), jnp.int32),
            pltpu.SMEM((margins,), jnp.int32),
            pltpu.SMEM((margins,), jnp.int32),
            pltpu.VMEM((fields, cells), F32),
            pltpu.VMEM((blocks, ROWS, LANES), F32),
            pltpu.VMEM((margins, EDGES, LANES), F32),
            pltpu.VMEM(remap_weights.shape[2:], BF16),
            pltpu.SemaphoreType.DMA((5,)),
        ],
        10**7,
    )(column_state[0, 0], mix, ver, *in_hbm(remap_weights, flux_coef, atm_block, ocean_block, tile_offset))
    mine, theirs, received, edge = call(
        functools.partial(rim_kernel, comps),
        (
            f32(REACH, blocks, fields, LANES),
            f32(REACH, blocks, fields, LANES),
            f32(blocks, fields, LANES),
            f32(fields, levels, LANES),
        ),
        [VMEM] * 7,
        [VMEM] * 4,
        [pltpu.VMEM((fields, LANES), F32)],
        10**6,
    )(from_left, from_right, own, coef, lean, buf, wide)
    mine = mine + swapped(theirs, "comp", 1)
    for step in range(REACH, 0, -1):
        arrived = sideways(mine[step - 1], step)
        received = received + arrived
    low, land, out = call(
        functools.partial(finish_kernel, comps),
        (
            f32(fields, ROWS, cells),
            f32(1, cells),
            jax.ShapeDtypeStruct(column_state.shape, F32),
        ),
        [VMEM] * 3 + [HBM] * 2,
        [VMEM, VMEM, HBM],
        [
            pltpu.VMEM((fields, levels - ROWS, cells), F32),
            pltpu.VMEM((fields, cells), F32),
            pltpu.VMEM(ocean_mask.shape, jnp.int32),
            pltpu.SMEM(flux_coef.shape, F32),
            pltpu.SemaphoreType.DMA((2 * fields + 2,)),
        ],
        10**7,
    )(field, edge, ver, *in_hbm(flux_coef, ocean_mask))
    received = gathered(received)
    out, _ = call(
        functools.partial(ocean_kernel, comps),
        (jax.ShapeDtypeStruct(column_state.shape, F32), f32(fields, ROWS, cells)),
        [HBM, VMEM, VMEM, VMEM],
        [HBM, VMEM],
        [pltpu.SemaphoreType.DMA((fields,))],
        10**6,
        aliases={0: 0, 1: 1},
    )(out, low, received, land)
    return out


def solution(mesh):
    placed = (
        P("comp", "tile", None, None, None),
        P(),
        P(),
        P(),
        P("comp", "tile", None),
        P("comp", "tile", None),
        P("comp", "tile", None),
        P("comp", "tile", None, None, None),
        P("tile", None),
    )
    return jax.shard_map(
        step,
        mesh=mesh,
        in_specs=placed,
        out_specs=P("comp", "tile", None, None, None),
        check_vma=False,
    )
```

```python
import functools

import jax
import jax.numpy as jnp
from jax import lax
from jax.experimental import pallas as pl
from jax.experimental.pallas import tpu as pltpu
from jax.sharding import PartitionSpec as P

REACH = 3
SUB = 2
TURNS = ((2, 3, -1), (1, -3, -2))
LANES = 128
ROWS = 8
MID = LANES // 2
EDGES = 2 * SUB
F32 = jnp.float32
BF16 = jnp.bfloat16
VMEM = pl.BlockSpec(memory_space=pltpu.VMEM)
HBM = pl.BlockSpec(memory_space=pltpu.HBM)


def moved(value, axis, steps):
    count = lax.axis_size(axis)
    return lax.ppermute(value, axis, [(i, (i + steps) % count) for i in range(count)])


def gathered(value):
    comps = lax.axis_size("comp")
    last = comps - 1
    if comps == 4:
        cycles = [(1, last, 0, 2), (0, last, 2, 1)]
        paths = [list(zip(c, c[1:] + c[:1])) for c in cycles]
        paths.append([(i, i ^ 1) for i in range(comps)])
    else:
        paths = [[(i, (i + s) % comps) for i in range(comps)] for s in range(1, comps)]
    total = value
    for pairs in paths:
        arrived = lax.ppermute(value, "comp", pairs)
        total = total + arrived
    return total


def swapped(value, axis, bit):
    count = lax.axis_size(axis)
    return lax.ppermute(value, axis, [(i, i ^ bit) for i in range(count)])


def sideways(value, turn):
    comps, tiles = lax.axis_size("comp"), lax.axis_size("tile")
    pairs = []
    for c in range(comps):
        shift = TURNS[c % 2][turn]
        pairs += [(c * tiles + t, c * tiles + (t + shift) % tiles) for t in range(tiles)]
    return lax.ppermute(value, ("comp", "tile"), pairs)


def in_hbm(*arrays):
    return [pltpu.with_memory_space_constraint(a, pltpu.HBM) for a in arrays]


def lanes_of(shape):
    return lax.broadcasted_iota(jnp.int32, shape, len(shape) - 1)


def turned(value, steps):
    width = value.shape[-1]
    steps = steps % width
    return value if steps == 0 else pltpu.roll(value, steps, axis=value.ndim - 1)


def atmosphere(comps):
    return lax.axis_index("comp") < comps - 1


def split(value):
    high = value.astype(BF16)
    return high, (value - high.astype(F32)).astype(BF16)


def product(vh, vl, field):
    high, low = split(field)
    dot = functools.partial(jnp.dot, preferred_element_type=F32)
    return dot(vh, high) + dot(vl, high) + dot(vh, low)


def stencil(coef, x):
    near = turned(x, 1) + turned(x, -1)
    far = turned(x, 2) + turned(x, -2)
    return coef[0] * x + coef[1] * near + coef[2] * far


def edges_kernel(comps, state, mixing, vertical, own, to_right, to_left, mix, ver, head, tail, sems):
    group = jnp.where(atmosphere(comps), 0, 1)
    cells = state.shape[-1]
    first = pltpu.make_async_copy(state.at[0, 0, :, :, pl.ds(0, LANES)], head, sems.at[0])
    last = pltpu.make_async_copy(state.at[0, 0, :, :, pl.ds(cells - LANES, LANES)], tail, sems.at[1])
    others = [
        pltpu.make_async_copy(mixing.at[group], mix, sems.at[2]),
        pltpu.make_async_copy(vertical.at[group], ver, sems.at[3]),
    ]
    for copy in [first, last] + others:
        copy.start()
    first.wait()
    last.wait()
    lane = lanes_of((ROWS, LANES))
    right = jnp.zeros((ROWS, LANES), F32)
    left = jnp.zeros((ROWS, LANES), F32)
    number = 0
    for k in range(head.shape[0]):
        for h in range(0, head.shape[1], ROWS):
            a, b = head[k, h : h + ROWS, :], tail[k, h : h + ROWS, :]
            at = SUB * number
            here = (lane >= at) & (lane < at + SUB)
            left = jnp.where(here, turned(a, at), left)
            right = jnp.where(here, turned(b, at + SUB), right)
            own[k, h : h + ROWS, :] = jnp.where(lane < MID, turned(a, SUB), turned(b, MID + 2 * SUB))
            number += 1
    to_right[...] = right
    to_left[...] = left
    for copy in others:
        copy.wait()


def column_of(row, square):
    eye = lax.broadcasted_iota(jnp.int32, square, 0) == lanes_of(square)
    return jnp.sum(jnp.where(eye, jnp.broadcast_to(row, square), 0.0), axis=1, keepdims=True)


def interior_kernel(
    comps,
    state,
    mix,
    ver,
    weights_hbm,
    flux,
    atm,
    ocean,
    offset,
    spread_out,
    buf,
    wide,
    coef,
    lean,
    flux_s,
    atm_s,
    ocean_s,
    offset_s,
    press,
    round_ref,
    rim,
    weights,
    sems,
):
    fields, levels, cells = state.shape
    blocks = cells // LANES
    copies = [
        pltpu.make_async_copy(src, dst, sems.at[i])
        for i, (src, dst) in enumerate(
            (
                (flux, flux_s),
                (atm.at[0, 0], atm_s),
                (ocean.at[0, 0], ocean_s),
                (offset.at[0, 0], offset_s),
                (weights_hbm.at[0, 0], weights),
            )
        )
    ]
    for copy in copies:
        copy.start()
    is_atmos = atmosphere(comps)
    right_core = lax.axis_index("comp") % 2
    buf[...] = jnp.zeros_like(buf)
    wide[...] = jnp.zeros_like(wide)
    square = (levels, levels)
    lane = lanes_of((1, levels))
    last = ver[levels - 1 : levels, :] + jnp.where(lane == levels - 1, 1.0, 0.0)
    second = ver[levels - 2 : levels - 1, :] + jnp.where(lane == levels - 2, 1.0, 0.0)
    last, second = column_of(last, square), column_of(second, square)
    for k in range(fields):
        rate = column_of(mix[k : k + 1, :], square)
        far = rate * rate
        near = 2.0 * rate - 4.0 * far
        mid = 1.0 - 4.0 * rate + 6.0 * far
        for i, c in enumerate((mid, near, far)):
            coef[i, k] = jnp.broadcast_to(c, (levels, LANES))
        spread_out[k] = stencil((mid, near, far), state[k])
    copies[0].wait()
    for k in range(fields):
        pull = flux_s[0, k] * last + flux_s[1, k] * second
        lean[k] = jnp.broadcast_to(pull, (levels, LANES))
        press[k : k + 1, :] = jnp.sum(pull * spread_out[k], axis=0, keepdims=True)
    surface = jnp.where(is_atmos, jnp.tanh(press[...]), 0.0).astype(BF16).astype(F32)
    lane = lanes_of((fields, LANES))
    round_ref[...] = jnp.zeros_like(round_ref)
    for b in range(blocks):
        value = surface[:, b * LANES : (b + 1) * LANES]
        if b == 0:
            value = jnp.where(lane < SUB, 0.0, value)
        if b == blocks - 1:
            value = jnp.where(lane >= LANES - SUB, 0.0, value)
        round_ref[b, :fields, :] = value
    for copy in copies[1:]:
        copy.wait()
    side = lax.broadcasted_iota(jnp.int32, (EDGES, LANES), 0) < SUB
    for n in range(weights.shape[0]):
        block = jnp.clip(atm_s[n], 0, blocks - 1)
        place = jnp.clip(ocean_s[n], 0, blocks - 1)
        distance = jnp.clip(offset_s[n], 0, 2 * REACH) - REACH
        slot = 2 * REACH
        for core in range(2):
            for turn in range(REACH):
                spot = jnp.where(right_core == core, turn, REACH + turn)
                slot = jnp.where(distance == TURNS[core][turn], spot, slot)
        term = jnp.dot(round_ref[block].astype(BF16), weights[n], preferred_element_type=F32)
        buf[slot, place] = buf[slot, place] + term[:fields]
        rim[n, :SUB, :] = weights[n, : 2 * ROWS, :].astype(F32)[:SUB]
        rim[n, SUB:, :] = weights[n, LANES - 2 * ROWS :, :].astype(F32)[2 * ROWS - SUB :]
        lead = jnp.where(block == 0, 1.0, 0.0)
        trail = jnp.where(block == blocks - 1, 1.0, 0.0)
        wide[slot, place] = wide[slot, place] + jnp.where(side, lead, trail) * rim[n]


def rim_kernel(
    comps, from_left, from_right, own, coef, lean, buf, wide, mine, theirs, here, edge, press
):
    fields, levels, _ = own.shape
    lane = lanes_of((ROWS, LANES))
    beyond = (lane >= MID + 2 * SUB) & (lane < MID + 3 * SUB)
    number = 0
    for k in range(fields):
        total = jnp.zeros((ROWS, LANES), F32)
        for h in range(0, levels, ROWS):
            at = SUB * number
            x = own[k, h : h + ROWS, :]
            x = jnp.where(lane < SUB, turned(from_left[...], -at), x)
            x = jnp.where(beyond, turned(from_right[...], MID + 2 * SUB - at), x)
            field = stencil([coef[i, k, h : h + ROWS, :] for i in range(3)], x)
            edge[k, h : h + ROWS, :] = field
            total = total + lean[k, h : h + ROWS, :] * field
            number += 1
        press[k : k + 1, :] = jnp.sum(total, axis=0, keepdims=True)
    value = jnp.where(atmosphere(comps), jnp.tanh(press[...]), 0.0).astype(BF16).astype(F32)
    spots = [SUB + i for i in range(SUB)] + [MID + SUB + i for i in range(SUB)]
    column = [jnp.broadcast_to(value[:, s : s + 1], (fields, LANES)) for s in spots]
    for slot in range(buf.shape[0]):
        for place in range(buf.shape[1]):
            total = buf[slot, place]
            for e in range(EDGES):
                total = total + column[e] * wide[slot, place, e : e + 1, :]
            if slot < REACH:
                mine[slot, place] = total
            elif slot < 2 * REACH:
                theirs[slot - REACH, place] = total
            else:
                here[place] = total


def finish_kernel(comps, field_in, edge, ver, flux, mask, low, land, out, high, press, raw, flux_s, sems):
    fields, levels, cells = field_in.shape
    copies = [
        pltpu.make_async_copy(mask, raw, sems.at[2 * fields]),
        pltpu.make_async_copy(flux, flux_s, sems.at[2 * fields + 1]),
    ]
    for copy in copies:
        copy.start()
    vh, vl = split(ver[...])
    lane = lanes_of((levels, LANES))
    is_atmos = atmosphere(comps)
    copies[1].wait()
    waits = [copies[0]]
    for k in range(fields):
        value = edge[k]
        first = jnp.where(lane < SUB, turned(value, -SUB), field_in[k, :, :LANES])
        last = jnp.where(lane >= LANES - SUB, turned(value, MID - 2 * SUB), field_in[k, :, cells - LANES :])
        field = jnp.concatenate([first, field_in[k, :, LANES : cells - LANES], last], axis=1)
        mixed = field + product(vh, vl, field)
        low[k] = mixed[:ROWS]
        high[k] = mixed[ROWS:]
        press[k : k + 1, :] = (
            flux_s[0, k] * mixed[levels - 1 : levels, :] + flux_s[1, k] * mixed[levels - 2 : levels - 1, :]
        )
        waits.append(pltpu.make_async_copy(low.at[k], out.at[0, 0, k, pl.ds(0, ROWS), :], sems.at[k]))
        waits[-1].start()
    press[...] = jnp.where(is_atmos, jnp.tanh(press[...]), 0.0)
    end = high.shape[1] - 1
    for k in range(fields):
        high[k, end : end + 1, :] = high[k, end : end + 1, :] - 0.5 * press[k : k + 1, :]
        waits.append(
            pltpu.make_async_copy(
                high.at[k], out.at[0, 0, k, pl.ds(ROWS, levels - ROWS), :], sems.at[fields + k]
            )
        )
        waits[-1].start()
    for copy in waits:
        copy.wait()
    land[...] = raw[...].astype(F32)


def ocean_kernel(comps, out_in, low_in, received, land, out, low, sems):
    fields, rows, cells = low.shape

    @pl.when(jnp.logical_not(atmosphere(comps)))
    def _():
        copies = []
        for k in range(fields):
            for b in range(cells // LANES):
                at = slice(b * LANES, (b + 1) * LANES)
                low[k, 0:1, at] = low_in[k, 0:1, at] + land[:, at] * received[b, k : k + 1, :]
            copies.append(
                pltpu.make_async_copy(low.at[k], out.at[0, 0, k, pl.ds(0, rows), :], sems.at[k])
            )
            copies[-1].start()
        for copy in copies:
            copy.wait()


def call(body, out_shape, in_specs, out_specs, scratch, flops, aliases=None):
    return pl.pallas_call(
        body,
        out_shape=out_shape,
        in_specs=in_specs,
        out_specs=out_specs,
        scratch_shapes=scratch,
        input_output_aliases=aliases or {},
        compiler_params=pltpu.CompilerParams(vmem_limit_bytes=16 << 20),
        cost_estimate=pl.CostEstimate(flops=flops, bytes_accessed=flops // 8, transcendentals=0),
    )


def step(
    column_state,
    mixing,
    vertical,
    flux_coef,
    atm_block,
    ocean_block,
    tile_offset,
    remap_weights,
    ocean_mask,
):
    _, _, fields, levels, cells = column_state.shape
    margins, across, ocean_cells = remap_weights.shape[2:]
    blocks = cells // LANES
    spread = 2 * REACH + 1
    comps = lax.axis_size("comp")
    groups = fields * levels // ROWS
    assert across == LANES and ocean_cells == LANES and levels == 2 * ROWS
    assert groups * SUB <= LANES and cells % LANES == 0

    def f32(*shape):
        return jax.ShapeDtypeStruct(shape, F32)

    own, to_right, to_left, mix, ver = call(
        functools.partial(edges_kernel, comps),
        (f32(fields, levels, LANES), f32(ROWS, LANES), f32(ROWS, LANES), f32(fields, levels), f32(levels, levels)),
        [HBM] * 3,
        [VMEM] * 5,
        [pltpu.VMEM((fields, levels, LANES), F32)] * 2 + [pltpu.SemaphoreType.DMA((4,))],
        10**5,
    )(*in_hbm(column_state, mixing, vertical))
    from_left = moved(to_right, "tile", 1)
    from_right = moved(to_left, "tile", -1)
    field, buf, wide, coef, lean = call(
        functools.partial(interior_kernel, comps),
        (
            f32(fields, levels, cells),
            f32(spread, blocks, fields, LANES),
            f32(spread, blocks, EDGES, LANES),
            f32(3, fields, levels, LANES),
            f32(fields, levels, LANES),
        ),
        [VMEM] * 3 + [HBM] * 5,
        [VMEM] * 5,
        [
            pltpu.SMEM(flux_coef.shape, F32),
            pltpu.SMEM((margins,), jnp.int32),
            pltpu.SMEM((margins,), jnp.int32),
            pltpu.SMEM((margins,), jnp.int32),
            pltpu.VMEM((fields, cells), F32),
            pltpu.VMEM((blocks, ROWS, LANES), F32),
            pltpu.VMEM((margins, EDGES, LANES), F32),
            pltpu.VMEM(remap_weights.shape[2:], BF16),
            pltpu.SemaphoreType.DMA((5,)),
        ],
        10**7,
    )(column_state[0, 0], mix, ver, *in_hbm(remap_weights, flux_coef, atm_block, ocean_block, tile_offset))
    mine, theirs, received, edge = call(
        functools.partial(rim_kernel, comps),
        (
            f32(REACH, blocks, fields, LANES),
            f32(REACH, blocks, fields, LANES),
            f32(blocks, fields, LANES),
            f32(fields, levels, LANES),
        ),
        [VMEM] * 7,
        [VMEM] * 4,
        [pltpu.VMEM((fields, LANES), F32)],
        10**6,
    )(from_left, from_right, own, coef, lean, buf, wide)
    mine = mine + swapped(theirs, "comp", 1)
    for turn in range(REACH):
        arrived = sideways(mine[turn], turn)
        received = received + arrived
    low, land, out = call(
        functools.partial(finish_kernel, comps),
        (
            f32(fields, ROWS, cells),
            f32(1, cells),
            jax.ShapeDtypeStruct(column_state.shape, F32),
        ),
        [VMEM] * 3 + [HBM] * 2,
        [VMEM, VMEM, HBM],
        [
            pltpu.VMEM((fields, levels - ROWS, cells), F32),
            pltpu.VMEM((fields, cells), F32),
            pltpu.VMEM(ocean_mask.shape, jnp.int32),
            pltpu.SMEM(flux_coef.shape, F32),
            pltpu.SemaphoreType.DMA((2 * fields + 2,)),
        ],
        10**7,
    )(field, edge, ver, *in_hbm(flux_coef, ocean_mask))
    received = gathered(received)
    out, _ = call(
        functools.partial(ocean_kernel, comps),
        (jax.ShapeDtypeStruct(column_state.shape, F32), f32(fields, ROWS, cells)),
        [HBM, VMEM, VMEM, VMEM],
        [HBM, VMEM],
        [pltpu.SemaphoreType.DMA((fields,))],
        10**6,
        aliases={0: 0, 1: 1},
    )(out, low, received, land)
    return out


def solution(mesh):
    placed = (
        P("comp", "tile", None, None, None),
        P(),
        P(),
        P(),
        P("comp", "tile", None),
        P("comp", "tile", None),
        P("comp", "tile", None),
        P("comp", "tile", None, None, None),
        P("tile", None),
    )
    return jax.shard_map(
        step,
        mesh=mesh,
        in_specs=placed,
        out_specs=P("comp", "tile", None, None, None),
        check_vma=False,
    )
```

```python
import functools

import jax
import jax.numpy as jnp
from jax import lax
from jax.experimental import pallas as pl
from jax.experimental.pallas import tpu as pltpu
from jax.sharding import PartitionSpec as P

REACH = 3
SUB = 2
TURNS = ((2, 3, -1), (1, -3, -2))
LANES = 128
ROWS = 8
MID = LANES // 2
EDGES = 2 * SUB
F32 = jnp.float32
BF16 = jnp.bfloat16
VMEM = pl.BlockSpec(memory_space=pltpu.VMEM)
HBM = pl.BlockSpec(memory_space=pltpu.HBM)


def moved(value, axis, steps):
    count = lax.axis_size(axis)
    return lax.ppermute(value, axis, [(i, (i + steps) % count) for i in range(count)])


def gathered(value):
    comps = lax.axis_size("comp")
    last = comps - 1
    if comps == 4:
        cycles = [(1, last, 0, 2), (0, last, 2, 1)]
        paths = [list(zip(c, c[1:] + c[:1])) for c in cycles]
        paths.append([(i, i ^ 1) for i in range(comps)])
    else:
        paths = [[(i, (i + s) % comps) for i in range(comps)] for s in range(1, comps)]
    total = value
    for pairs in paths:
        arrived = lax.ppermute(value, "comp", pairs)
        total = total + arrived
    return total


def swapped(value, axis, bit):
    count = lax.axis_size(axis)
    return lax.ppermute(value, axis, [(i, i ^ bit) for i in range(count)])


def sideways(value, turn):
    comps, tiles = lax.axis_size("comp"), lax.axis_size("tile")
    pairs = []
    for c in range(comps):
        shift = TURNS[c % 2][turn]
        pairs += [(c * tiles + t, c * tiles + (t + shift) % tiles) for t in range(tiles)]
    return lax.ppermute(value, ("comp", "tile"), pairs)


def in_hbm(*arrays):
    return [pltpu.with_memory_space_constraint(a, pltpu.HBM) for a in arrays]


def lanes_of(shape):
    return lax.broadcasted_iota(jnp.int32, shape, len(shape) - 1)


def turned(value, steps):
    width = value.shape[-1]
    steps = steps % width
    return value if steps == 0 else pltpu.roll(value, steps, axis=value.ndim - 1)


def atmosphere(comps):
    return lax.axis_index("comp") < comps - 1


def split(value):
    high = value.astype(BF16)
    return high, (value - high.astype(F32)).astype(BF16)


def product(vh, vl, field):
    high, low = split(field)
    dot = functools.partial(jnp.dot, preferred_element_type=F32)
    return dot(vh, high) + dot(vl, high) + dot(vh, low)


def stencil(coef, x):
    near = turned(x, 1) + turned(x, -1)
    far = turned(x, 2) + turned(x, -2)
    return coef[0] * x + coef[1] * near + coef[2] * far


def edges_kernel(comps, state, mixing, vertical, own, to_right, to_left, mix, ver, head, tail, sems):
    group = jnp.where(atmosphere(comps), 0, 1)
    cells = state.shape[-1]
    first = pltpu.make_async_copy(state.at[0, 0, :, :, pl.ds(0, LANES)], head, sems.at[0])
    last = pltpu.make_async_copy(state.at[0, 0, :, :, pl.ds(cells - LANES, LANES)], tail, sems.at[1])
    others = [
        pltpu.make_async_copy(mixing.at[group], mix, sems.at[2]),
        pltpu.make_async_copy(vertical.at[group], ver, sems.at[3]),
    ]
    for copy in [first, last] + others:
        copy.start()
    first.wait()
    last.wait()
    lane = lanes_of((ROWS, LANES))
    right = jnp.zeros((ROWS, LANES), F32)
    left = jnp.zeros((ROWS, LANES), F32)
    number = 0
    for k in range(head.shape[0]):
        for h in range(0, head.shape[1], ROWS):
            a, b = head[k, h : h + ROWS, :], tail[k, h : h + ROWS, :]
            at = SUB * number
            here = (lane >= at) & (lane < at + SUB)
            left = jnp.where(here, turned(a, at), left)
            right = jnp.where(here, turned(b, at + SUB), right)
            own[k, h : h + ROWS, :] = jnp.where(lane < MID, turned(a, SUB), turned(b, MID + 2 * SUB))
            number += 1
    to_right[...] = right
    to_left[...] = left
    for copy in others:
        copy.wait()


def column_of(row, square):
    eye = lax.broadcasted_iota(jnp.int32, square, 0) == lanes_of(square)
    return jnp.sum(jnp.where(eye, jnp.broadcast_to(row, square), 0.0), axis=1, keepdims=True)


def interior_kernel(
    comps,
    state,
    mix,
    ver,
    weights_hbm,
    flux,
    atm,
    ocean,
    offset,
    spread_out,
    buf,
    wide,
    coef,
    lean,
    flux_s,
    atm_s,
    ocean_s,
    offset_s,
    press,
    round_ref,
    rim,
    weights,
    sems,
):
    fields, levels, cells = state.shape
    blocks = cells // LANES
    copies = [
        pltpu.make_async_copy(src, dst, sems.at[i])
        for i, (src, dst) in enumerate(
            (
                (flux, flux_s),
                (atm.at[0, 0], atm_s),
                (ocean.at[0, 0], ocean_s),
                (offset.at[0, 0], offset_s),
                (weights_hbm.at[0, 0], weights),
            )
        )
    ]
    for copy in copies:
        copy.start()
    is_atmos = atmosphere(comps)
    right_core = lax.axis_index("comp") % 2
    buf[...] = jnp.zeros_like(buf)
    wide[...] = jnp.zeros_like(wide)
    square = (levels, levels)
    lane = lanes_of((1, levels))
    last = ver[levels - 1 : levels, :] + jnp.where(lane == levels - 1, 1.0, 0.0)
    second = ver[levels - 2 : levels - 1, :] + jnp.where(lane == levels - 2, 1.0, 0.0)
    last, second = column_of(last, square), column_of(second, square)
    for k in range(fields):
        rate = column_of(mix[k : k + 1, :], square)
        far = rate * rate
        near = 2.0 * rate - 4.0 * far
        mid = 1.0 - 4.0 * rate + 6.0 * far
        for i, c in enumerate((mid, near, far)):
            coef[i, k] = jnp.broadcast_to(c, (levels, LANES))
        spread_out[k] = stencil((mid, near, far), state[k])
    copies[0].wait()
    for k in range(fields):
        pull = flux_s[0, k] * last + flux_s[1, k] * second
        lean[k] = jnp.broadcast_to(pull, (levels, LANES))
        press[k : k + 1, :] = jnp.sum(pull * spread_out[k], axis=0, keepdims=True)
    surface = jnp.where(is_atmos, jnp.tanh(press[...]), 0.0).astype(BF16).astype(F32)
    lane = lanes_of((fields, LANES))
    round_ref[...] = jnp.zeros_like(round_ref)
    for b in range(blocks):
        value = surface[:, b * LANES : (b + 1) * LANES]
        if b == 0:
            value = jnp.where(lane < SUB, 0.0, value)
        if b == blocks - 1:
            value = jnp.where(lane >= LANES - SUB, 0.0, value)
        round_ref[b, :fields, :] = value
    for copy in copies[1:]:
        copy.wait()
    side = lax.broadcasted_iota(jnp.int32, (EDGES, LANES), 0) < SUB
    for n in range(weights.shape[0]):
        block = jnp.clip(atm_s[n], 0, blocks - 1)
        place = jnp.clip(ocean_s[n], 0, blocks - 1)
        distance = jnp.clip(offset_s[n], 0, 2 * REACH) - REACH
        slot = 2 * REACH
        for core in range(2):
            for turn in range(REACH):
                spot = jnp.where(right_core == core, turn, REACH + turn)
                slot = jnp.where(distance == TURNS[core][turn], spot, slot)
        term = jnp.dot(round_ref[block].astype(BF16), weights[n], preferred_element_type=F32)
        buf[slot, place] = buf[slot, place] + term[:fields]
        rim[n, :SUB, :] = weights[n, : 2 * ROWS, :].astype(F32)[:SUB]
        rim[n, SUB:, :] = weights[n, LANES - 2 * ROWS :, :].astype(F32)[2 * ROWS - SUB :]
        lead = jnp.where(block == 0, 1.0, 0.0)
        trail = jnp.where(block == blocks - 1, 1.0, 0.0)
        wide[slot, place] = wide[slot, place] + jnp.where(side, lead, trail) * rim[n]


def rim_kernel(
    comps, from_left, from_right, own, coef, lean, buf, wide, theirs, edge, value, press
):
    fields, levels, _ = own.shape
    lane = lanes_of((ROWS, LANES))
    beyond = (lane >= MID + 2 * SUB) & (lane < MID + 3 * SUB)
    number = 0
    for k in range(fields):
        total = jnp.zeros((ROWS, LANES), F32)
        for h in range(0, levels, ROWS):
            at = SUB * number
            x = own[k, h : h + ROWS, :]
            x = jnp.where(lane < SUB, turned(from_left[...], -at), x)
            x = jnp.where(beyond, turned(from_right[...], MID + 2 * SUB - at), x)
            field = stencil([coef[i, k, h : h + ROWS, :] for i in range(3)], x)
            edge[k, h : h + ROWS, :] = field
            total = total + lean[k, h : h + ROWS, :] * field
            number += 1
        press[k : k + 1, :] = jnp.sum(total, axis=0, keepdims=True)
    surface = jnp.where(atmosphere(comps), jnp.tanh(press[...]), 0.0).astype(BF16).astype(F32)
    value[...] = surface
    added(surface, buf, wide, [(theirs, turn, REACH + turn) for turn in range(REACH)])


def added(surface, buf, wide, moves):
    fields, _ = surface.shape
    spots = [SUB + i for i in range(SUB)] + [MID + SUB + i for i in range(SUB)]
    column = [jnp.broadcast_to(surface[:, s : s + 1], (fields, LANES)) for s in spots]
    for target, turn, slot in moves:
        for place in range(buf.shape[1]):
            total = buf[slot, place]
            for e in range(EDGES):
                total = total + column[e] * wide[slot, place, e : e + 1, :]
            target[turn, place] = total


def mine_kernel(value, buf, wide, mine, here):
    moves = [(mine, turn, turn) for turn in range(REACH)] + [(here, 0, 2 * REACH)]
    added(value[...], buf, wide, moves)


def finish_kernel(comps, field_in, edge, ver, flux, mask, low, land, out, high, press, raw, flux_s, sems):
    fields, levels, cells = field_in.shape
    copies = [
        pltpu.make_async_copy(mask, raw, sems.at[2 * fields]),
        pltpu.make_async_copy(flux, flux_s, sems.at[2 * fields + 1]),
    ]
    for copy in copies:
        copy.start()
    vh, vl = split(ver[...])
    lane = lanes_of((levels, LANES))
    is_atmos = atmosphere(comps)
    copies[1].wait()
    waits = [copies[0]]
    for k in range(fields):
        value = edge[k]
        first = jnp.where(lane < SUB, turned(value, -SUB), field_in[k, :, :LANES])
        last = jnp.where(lane >= LANES - SUB, turned(value, MID - 2 * SUB), field_in[k, :, cells - LANES :])
        field = jnp.concatenate([first, field_in[k, :, LANES : cells - LANES], last], axis=1)
        mixed = field + product(vh, vl, field)
        low[k] = mixed[:ROWS]
        high[k] = mixed[ROWS:]
        press[k : k + 1, :] = (
            flux_s[0, k] * mixed[levels - 1 : levels, :] + flux_s[1, k] * mixed[levels - 2 : levels - 1, :]
        )
        waits.append(pltpu.make_async_copy(low.at[k], out.at[0, 0, k, pl.ds(0, ROWS), :], sems.at[k]))
        waits[-1].start()
    press[...] = jnp.where(is_atmos, jnp.tanh(press[...]), 0.0)
    end = high.shape[1] - 1
    for k in range(fields):
        high[k, end : end + 1, :] = high[k, end : end + 1, :] - 0.5 * press[k : k + 1, :]
        waits.append(
            pltpu.make_async_copy(
                high.at[k], out.at[0, 0, k, pl.ds(ROWS, levels - ROWS), :], sems.at[fields + k]
            )
        )
        waits[-1].start()
    for copy in waits:
        copy.wait()
    land[...] = raw[...].astype(F32)


def ocean_kernel(comps, out_in, low, received, land, out, row, sems):
    fields, _, cells = low.shape

    @pl.when(jnp.logical_not(atmosphere(comps)))
    def _():
        copies = []
        for k in range(fields):
            for b in range(cells // LANES):
                at = slice(b * LANES, (b + 1) * LANES)
                row[k, 0:1, at] = low[k, 0:1, at] + land[:, at] * received[b, k : k + 1, :]
            copies.append(pltpu.make_async_copy(row.at[k], out.at[0, 0, k, pl.ds(0, 1), :], sems.at[k]))
            copies[-1].start()
        for copy in copies:
            copy.wait()


def call(body, out_shape, in_specs, out_specs, scratch, flops, aliases=None):
    return pl.pallas_call(
        body,
        out_shape=out_shape,
        in_specs=in_specs,
        out_specs=out_specs,
        scratch_shapes=scratch,
        input_output_aliases=aliases or {},
        compiler_params=pltpu.CompilerParams(vmem_limit_bytes=16 << 20),
        cost_estimate=pl.CostEstimate(flops=flops, bytes_accessed=flops // 8, transcendentals=0),
    )


def step(
    column_state,
    mixing,
    vertical,
    flux_coef,
    atm_block,
    ocean_block,
    tile_offset,
    remap_weights,
    ocean_mask,
):
    _, _, fields, levels, cells = column_state.shape
    margins, across, ocean_cells = remap_weights.shape[2:]
    blocks = cells // LANES
    spread = 2 * REACH + 1
    comps = lax.axis_size("comp")
    groups = fields * levels // ROWS
    assert across == LANES and ocean_cells == LANES and levels == 2 * ROWS
    assert groups * SUB <= LANES and cells % LANES == 0

    def f32(*shape):
        return jax.ShapeDtypeStruct(shape, F32)

    own, to_right, to_left, mix, ver = call(
        functools.partial(edges_kernel, comps),
        (f32(fields, levels, LANES), f32(ROWS, LANES), f32(ROWS, LANES), f32(fields, levels), f32(levels, levels)),
        [HBM] * 3,
        [VMEM] * 5,
        [pltpu.VMEM((fields, levels, LANES), F32)] * 2 + [pltpu.SemaphoreType.DMA((4,))],
        10**5,
    )(*in_hbm(column_state, mixing, vertical))
    from_left = moved(to_right, "tile", 1)
    from_right = moved(to_left, "tile", -1)
    field, buf, wide, coef, lean = call(
        functools.partial(interior_kernel, comps),
        (
            f32(fields, levels, cells),
            f32(spread, blocks, fields, LANES),
            f32(spread, blocks, EDGES, LANES),
            f32(3, fields, levels, LANES),
            f32(fields, levels, LANES),
        ),
        [VMEM] * 3 + [HBM] * 5,
        [VMEM] * 5,
        [
            pltpu.SMEM(flux_coef.shape, F32),
            pltpu.SMEM((margins,), jnp.int32),
            pltpu.SMEM((margins,), jnp.int32),
            pltpu.SMEM((margins,), jnp.int32),
            pltpu.VMEM((fields, cells), F32),
            pltpu.VMEM((blocks, ROWS, LANES), F32),
            pltpu.VMEM((margins, EDGES, LANES), F32),
            pltpu.VMEM(remap_weights.shape[2:], BF16),
            pltpu.SemaphoreType.DMA((5,)),
        ],
        10**7,
    )(column_state[0, 0], mix, ver, *in_hbm(remap_weights, flux_coef, atm_block, ocean_block, tile_offset))
    theirs, edge, value = call(
        functools.partial(rim_kernel, comps),
        (f32(REACH, blocks, fields, LANES), f32(fields, levels, LANES), f32(fields, LANES)),
        [VMEM] * 7,
        [VMEM] * 3,
        [pltpu.VMEM((fields, LANES), F32)],
        10**6,
    )(from_left, from_right, own, coef, lean, buf, wide)
    swap = swapped(theirs, "comp", 1)
    mine, received = call(
        mine_kernel,
        (f32(REACH, blocks, fields, LANES), f32(1, blocks, fields, LANES)),
        [VMEM] * 3,
        [VMEM] * 2,
        [],
        10**6,
    )(value, buf, wide)
    mine = mine + swap
    received = received[0]
    for turn in range(REACH):
        arrived = sideways(mine[turn], turn)
        received = received + arrived
    low, land, out = call(
        functools.partial(finish_kernel, comps),
        (
            f32(fields, ROWS, cells),
            f32(1, cells),
            jax.ShapeDtypeStruct(column_state.shape, F32),
        ),
        [VMEM] * 3 + [HBM] * 2,
        [VMEM, VMEM, HBM],
        [
            pltpu.VMEM((fields, levels - ROWS, cells), F32),
            pltpu.VMEM((fields, cells), F32),
            pltpu.VMEM(ocean_mask.shape, jnp.int32),
            pltpu.SMEM(flux_coef.shape, F32),
            pltpu.SemaphoreType.DMA((2 * fields + 2,)),
        ],
        10**7,
    )(field, edge, ver, *in_hbm(flux_coef, ocean_mask))
    received = gathered(received)
    return call(
        functools.partial(ocean_kernel, comps),
        jax.ShapeDtypeStruct(column_state.shape, F32),
        [HBM, VMEM, VMEM, VMEM],
        HBM,
        [pltpu.VMEM((fields, 1, cells), F32), pltpu.SemaphoreType.DMA((fields,))],
        10**6,
        aliases={0: 0},
    )(out, low, received, land)


def solution(mesh):
    placed = (
        P("comp", "tile", None, None, None),
        P(),
        P(),
        P(),
        P("comp", "tile", None),
        P("comp", "tile", None),
        P("comp", "tile", None),
        P("comp", "tile", None, None, None),
        P("tile", None),
    )
    return jax.shard_map(
        step,
        mesh=mesh,
        in_specs=placed,
        out_specs=P("comp", "tile", None, None, None),
        check_vma=False,
    )
```

```python
import functools

import jax
import jax.numpy as jnp
from jax import lax
from jax.experimental import pallas as pl
from jax.experimental.pallas import tpu as pltpu
from jax.sharding import PartitionSpec as P

REACH = 3
SUB = 2
TURNS = ((('R', 2), ('R', 1), ('R', -1)), (('A', 3), ('B', 3), ('R', -2)))
LANES = 128
ROWS = 8
MID = LANES // 2
EDGES = 2 * SUB
F32 = jnp.float32
BF16 = jnp.bfloat16
VMEM = pl.BlockSpec(memory_space=pltpu.VMEM)
HBM = pl.BlockSpec(memory_space=pltpu.HBM)


def moved(value, axis, steps):
    count = lax.axis_size(axis)
    return lax.ppermute(value, axis, [(i, (i + steps) % count) for i in range(count)])


def gathered(value):
    comps = lax.axis_size("comp")
    last = comps - 1
    if comps == 4:
        cycles = [(1, last, 0, 2), (0, last, 2, 1)]
        paths = [list(zip(c, c[1:] + c[:1])) for c in cycles]
        paths.append([(i, i ^ 1) for i in range(comps)])
    else:
        paths = [[(i, (i + s) % comps) for i in range(comps)] for s in range(1, comps)]
    total = value
    for pairs in paths:
        arrived = lax.ppermute(value, "comp", pairs)
        total = total + arrived
    return total


def swapped(value, axis, bit):
    count = lax.axis_size(axis)
    return lax.ppermute(value, axis, [(i, i ^ bit) for i in range(count)])


def displaced(kind, distance, tile):
    if kind == "R":
        return distance
    step = distance & -distance
    flip = (tile // step) % 2
    sign = 1 - 2 * flip if kind == "A" else 2 * flip - 1
    return sign * distance


def sideways(value, turn):
    comps, tiles = lax.axis_size("comp"), lax.axis_size("tile")
    pairs = []
    for c in range(comps):
        turns = [displaced(*TURNS[c % 2][turn], t) for t in range(tiles)]
        pairs += [(c * tiles + t, c * tiles + (t + turns[t]) % tiles) for t in range(tiles)]
    assert len({target for _, target in pairs}) == len(pairs)
    return lax.ppermute(value, ("comp", "tile"), pairs)


def in_hbm(*arrays):
    return [pltpu.with_memory_space_constraint(a, pltpu.HBM) for a in arrays]


def lanes_of(shape):
    return lax.broadcasted_iota(jnp.int32, shape, len(shape) - 1)


def turned(value, steps):
    width = value.shape[-1]
    steps = steps % width
    return value if steps == 0 else pltpu.roll(value, steps, axis=value.ndim - 1)


def atmosphere(comps):
    return lax.axis_index("comp") < comps - 1


def split(value):
    high = value.astype(BF16)
    return high, (value - high.astype(F32)).astype(BF16)


def product(vh, vl, field):
    high, low = split(field)
    dot = functools.partial(jnp.dot, preferred_element_type=F32)
    return dot(vh, high) + dot(vl, high) + dot(vh, low)


def stencil(coef, x):
    near = turned(x, 1) + turned(x, -1)
    far = turned(x, 2) + turned(x, -2)
    return coef[0] * x + coef[1] * near + coef[2] * far


def edges_kernel(comps, state, mixing, vertical, own, to_right, to_left, mix, ver, head, tail, sems):
    group = jnp.where(atmosphere(comps), 0, 1)
    cells = state.shape[-1]
    first = pltpu.make_async_copy(state.at[0, 0, :, :, pl.ds(0, LANES)], head, sems.at[0])
    last = pltpu.make_async_copy(state.at[0, 0, :, :, pl.ds(cells - LANES, LANES)], tail, sems.at[1])
    others = [
        pltpu.make_async_copy(mixing.at[group], mix, sems.at[2]),
        pltpu.make_async_copy(vertical.at[group], ver, sems.at[3]),
    ]
    for copy in [first, last] + others:
        copy.start()
    first.wait()
    last.wait()
    lane = lanes_of((ROWS, LANES))
    right = jnp.zeros((ROWS, LANES), F32)
    left = jnp.zeros((ROWS, LANES), F32)
    number = 0
    for k in range(head.shape[0]):
        for h in range(0, head.shape[1], ROWS):
            a, b = head[k, h : h + ROWS, :], tail[k, h : h + ROWS, :]
            at = SUB * number
            here = (lane >= at) & (lane < at + SUB)
            left = jnp.where(here, turned(a, at), left)
            right = jnp.where(here, turned(b, at + SUB), right)
            own[k, h : h + ROWS, :] = jnp.where(lane < MID, turned(a, SUB), turned(b, MID + 2 * SUB))
            number += 1
    to_right[...] = right
    to_left[...] = left
    for copy in others:
        copy.wait()


def column_of(row, square):
    eye = lax.broadcasted_iota(jnp.int32, square, 0) == lanes_of(square)
    return jnp.sum(jnp.where(eye, jnp.broadcast_to(row, square), 0.0), axis=1, keepdims=True)


def interior_kernel(
    comps,
    state,
    mix,
    ver,
    weights_hbm,
    flux,
    atm,
    ocean,
    offset,
    spread_out,
    buf,
    wide,
    coef,
    lean,
    flux_s,
    atm_s,
    ocean_s,
    offset_s,
    press,
    round_ref,
    rim,
    weights,
    sems,
):
    fields, levels, cells = state.shape
    blocks = cells // LANES
    copies = [
        pltpu.make_async_copy(src, dst, sems.at[i])
        for i, (src, dst) in enumerate(
            (
                (flux, flux_s),
                (atm.at[0, 0], atm_s),
                (ocean.at[0, 0], ocean_s),
                (offset.at[0, 0], offset_s),
                (weights_hbm.at[0, 0], weights),
            )
        )
    ]
    for copy in copies:
        copy.start()
    is_atmos = atmosphere(comps)
    right_core = lax.axis_index("comp") % 2
    tile = lax.axis_index("tile")
    buf[...] = jnp.zeros_like(buf)
    wide[...] = jnp.zeros_like(wide)
    square = (levels, levels)
    lane = lanes_of((1, levels))
    last = ver[levels - 1 : levels, :] + jnp.where(lane == levels - 1, 1.0, 0.0)
    second = ver[levels - 2 : levels - 1, :] + jnp.where(lane == levels - 2, 1.0, 0.0)
    last, second = column_of(last, square), column_of(second, square)
    for k in range(fields):
        rate = column_of(mix[k : k + 1, :], square)
        far = rate * rate
        near = 2.0 * rate - 4.0 * far
        mid = 1.0 - 4.0 * rate + 6.0 * far
        for i, c in enumerate((mid, near, far)):
            coef[i, k] = jnp.broadcast_to(c, (levels, LANES))
        spread_out[k] = stencil((mid, near, far), state[k])
    copies[0].wait()
    for k in range(fields):
        pull = flux_s[0, k] * last + flux_s[1, k] * second
        lean[k] = jnp.broadcast_to(pull, (levels, LANES))
        press[k : k + 1, :] = jnp.sum(pull * spread_out[k], axis=0, keepdims=True)
    surface = jnp.where(is_atmos, jnp.tanh(press[...]), 0.0).astype(BF16).astype(F32)
    lane = lanes_of((fields, LANES))
    round_ref[...] = jnp.zeros_like(round_ref)
    for b in range(blocks):
        value = surface[:, b * LANES : (b + 1) * LANES]
        if b == 0:
            value = jnp.where(lane < SUB, 0.0, value)
        if b == blocks - 1:
            value = jnp.where(lane >= LANES - SUB, 0.0, value)
        round_ref[b, :fields, :] = value
    for copy in copies[1:]:
        copy.wait()
    side = lax.broadcasted_iota(jnp.int32, (EDGES, LANES), 0) < SUB
    for n in range(weights.shape[0]):
        block = jnp.clip(atm_s[n], 0, blocks - 1)
        place = jnp.clip(ocean_s[n], 0, blocks - 1)
        distance = jnp.clip(offset_s[n], 0, 2 * REACH) - REACH
        slot = 2 * REACH
        for core in range(2):
            for turn in range(REACH):
                spot = jnp.where(right_core == core, turn, REACH + turn)
                slot = jnp.where(distance == displaced(*TURNS[core][turn], tile), spot, slot)
        term = jnp.dot(round_ref[block].astype(BF16), weights[n], preferred_element_type=F32)
        buf[slot, place] = buf[slot, place] + term[:fields]
        rim[n, :SUB, :] = weights[n, : 2 * ROWS, :].astype(F32)[:SUB]
        rim[n, SUB:, :] = weights[n, LANES - 2 * ROWS :, :].astype(F32)[2 * ROWS - SUB :]
        lead = jnp.where(block == 0, 1.0, 0.0)
        trail = jnp.where(block == blocks - 1, 1.0, 0.0)
        wide[slot, place] = wide[slot, place] + jnp.where(side, lead, trail) * rim[n]


def rim_kernel(
    comps, from_left, from_right, own, coef, lean, buf, wide, theirs, edge, value, press
):
    fields, levels, _ = own.shape
    lane = lanes_of((ROWS, LANES))
    beyond = (lane >= MID + 2 * SUB) & (lane < MID + 3 * SUB)
    number = 0
    for k in range(fields):
        total = jnp.zeros((ROWS, LANES), F32)
        for h in range(0, levels, ROWS):
            at = SUB * number
            x = own[k, h : h + ROWS, :]
            x = jnp.where(lane < SUB, turned(from_left[...], -at), x)
            x = jnp.where(beyond, turned(from_right[...], MID + 2 * SUB - at), x)
            field = stencil([coef[i, k, h : h + ROWS, :] for i in range(3)], x)
            edge[k, h : h + ROWS, :] = field
            total = total + lean[k, h : h + ROWS, :] * field
            number += 1
        press[k : k + 1, :] = jnp.sum(total, axis=0, keepdims=True)
    surface = jnp.where(atmosphere(comps), jnp.tanh(press[...]), 0.0).astype(BF16).astype(F32)
    value[...] = surface
    added(surface, buf, wide, [(theirs, turn, REACH + turn) for turn in range(REACH)])


def added(surface, buf, wide, moves):
    fields, _ = surface.shape
    spots = [SUB + i for i in range(SUB)] + [MID + SUB + i for i in range(SUB)]
    column = [jnp.broadcast_to(surface[:, s : s + 1], (fields, LANES)) for s in spots]
    for target, turn, slot in moves:
        for place in range(buf.shape[1]):
            total = buf[slot, place]
            for e in range(EDGES):
                total = total + column[e] * wide[slot, place, e : e + 1, :]
            target[turn, place] = total


def mine_kernel(value, buf, wide, mine, here):
    moves = [(mine, turn, turn) for turn in range(REACH)] + [(here, 0, 2 * REACH)]
    added(value[...], buf, wide, moves)


def finish_kernel(comps, field_in, edge, ver, flux, mask, low, land, out, high, press, raw, flux_s, sems):
    fields, levels, cells = field_in.shape
    copies = [
        pltpu.make_async_copy(mask, raw, sems.at[2 * fields]),
        pltpu.make_async_copy(flux, flux_s, sems.at[2 * fields + 1]),
    ]
    for copy in copies:
        copy.start()
    vh, vl = split(ver[...])
    lane = lanes_of((levels, LANES))
    is_atmos = atmosphere(comps)
    copies[1].wait()
    waits = [copies[0]]
    for k in range(fields):
        value = edge[k]
        first = jnp.where(lane < SUB, turned(value, -SUB), field_in[k, :, :LANES])
        last = jnp.where(lane >= LANES - SUB, turned(value, MID - 2 * SUB), field_in[k, :, cells - LANES :])
        field = jnp.concatenate([first, field_in[k, :, LANES : cells - LANES], last], axis=1)
        mixed = field + product(vh, vl, field)
        low[k] = mixed[:ROWS]
        high[k] = mixed[ROWS:]
        press[k : k + 1, :] = (
            flux_s[0, k] * mixed[levels - 1 : levels, :] + flux_s[1, k] * mixed[levels - 2 : levels - 1, :]
        )
        waits.append(pltpu.make_async_copy(low.at[k], out.at[0, 0, k, pl.ds(0, ROWS), :], sems.at[k]))
        waits[-1].start()
    press[...] = jnp.where(is_atmos, jnp.tanh(press[...]), 0.0)
    end = high.shape[1] - 1
    for k in range(fields):
        high[k, end : end + 1, :] = high[k, end : end + 1, :] - 0.5 * press[k : k + 1, :]
        waits.append(
            pltpu.make_async_copy(
                high.at[k], out.at[0, 0, k, pl.ds(ROWS, levels - ROWS), :], sems.at[fields + k]
            )
        )
        waits[-1].start()
    for copy in waits:
        copy.wait()
    land[...] = raw[...].astype(F32)


def ocean_kernel(comps, out_in, low, received, land, out, row, sems):
    fields, _, cells = low.shape

    @pl.when(jnp.logical_not(atmosphere(comps)))
    def _():
        copies = []
        for k in range(fields):
            for b in range(cells // LANES):
                at = slice(b * LANES, (b + 1) * LANES)
                row[k, 0:1, at] = low[k, 0:1, at] + land[:, at] * received[b, k : k + 1, :]
            copies.append(pltpu.make_async_copy(row.at[k], out.at[0, 0, k, pl.ds(0, 1), :], sems.at[k]))
            copies[-1].start()
        for copy in copies:
            copy.wait()


def call(body, out_shape, in_specs, out_specs, scratch, flops, aliases=None):
    return pl.pallas_call(
        body,
        out_shape=out_shape,
        in_specs=in_specs,
        out_specs=out_specs,
        scratch_shapes=scratch,
        input_output_aliases=aliases or {},
        compiler_params=pltpu.CompilerParams(vmem_limit_bytes=16 << 20),
        cost_estimate=pl.CostEstimate(flops=flops, bytes_accessed=flops // 8, transcendentals=0),
    )


def step(
    column_state,
    mixing,
    vertical,
    flux_coef,
    atm_block,
    ocean_block,
    tile_offset,
    remap_weights,
    ocean_mask,
):
    _, _, fields, levels, cells = column_state.shape
    margins, across, ocean_cells = remap_weights.shape[2:]
    blocks = cells // LANES
    spread = 2 * REACH + 1
    comps = lax.axis_size("comp")
    groups = fields * levels // ROWS
    assert across == LANES and ocean_cells == LANES and levels == 2 * ROWS
    assert groups * SUB <= LANES and cells % LANES == 0

    def f32(*shape):
        return jax.ShapeDtypeStruct(shape, F32)

    own, to_right, to_left, mix, ver = call(
        functools.partial(edges_kernel, comps),
        (f32(fields, levels, LANES), f32(ROWS, LANES), f32(ROWS, LANES), f32(fields, levels), f32(levels, levels)),
        [HBM] * 3,
        [VMEM] * 5,
        [pltpu.VMEM((fields, levels, LANES), F32)] * 2 + [pltpu.SemaphoreType.DMA((4,))],
        10**5,
    )(*in_hbm(column_state, mixing, vertical))
    from_left = moved(to_right, "tile", 1)
    from_right = moved(to_left, "tile", -1)
    field, buf, wide, coef, lean = call(
        functools.partial(interior_kernel, comps),
        (
            f32(fields, levels, cells),
            f32(spread, blocks, fields, LANES),
            f32(spread, blocks, EDGES, LANES),
            f32(3, fields, levels, LANES),
            f32(fields, levels, LANES),
        ),
        [VMEM] * 3 + [HBM] * 5,
        [VMEM] * 5,
        [
            pltpu.SMEM(flux_coef.shape, F32),
            pltpu.SMEM((margins,), jnp.int32),
            pltpu.SMEM((margins,), jnp.int32),
            pltpu.SMEM((margins,), jnp.int32),
            pltpu.VMEM((fields, cells), F32),
            pltpu.VMEM((blocks, ROWS, LANES), F32),
            pltpu.VMEM((margins, EDGES, LANES), F32),
            pltpu.VMEM(remap_weights.shape[2:], BF16),
            pltpu.SemaphoreType.DMA((5,)),
        ],
        10**7,
    )(column_state[0, 0], mix, ver, *in_hbm(remap_weights, flux_coef, atm_block, ocean_block, tile_offset))
    theirs, edge, value = call(
        functools.partial(rim_kernel, comps),
        (f32(REACH, blocks, fields, LANES), f32(fields, levels, LANES), f32(fields, LANES)),
        [VMEM] * 7,
        [VMEM] * 3,
        [pltpu.VMEM((fields, LANES), F32)],
        10**6,
    )(from_left, from_right, own, coef, lean, buf, wide)
    swap = swapped(theirs, "comp", 1)
    mine, received = call(
        mine_kernel,
        (f32(REACH, blocks, fields, LANES), f32(1, blocks, fields, LANES)),
        [VMEM] * 3,
        [VMEM] * 2,
        [],
        10**6,
    )(value, buf, wide)
    mine = mine + swap
    received = received[0]
    for turn in range(REACH):
        arrived = sideways(mine[turn], turn)
        received = received + arrived
    low, land, out = call(
        functools.partial(finish_kernel, comps),
        (
            f32(fields, ROWS, cells),
            f32(1, cells),
            jax.ShapeDtypeStruct(column_state.shape, F32),
        ),
        [VMEM] * 3 + [HBM] * 2,
        [VMEM, VMEM, HBM],
        [
            pltpu.VMEM((fields, levels - ROWS, cells), F32),
            pltpu.VMEM((fields, cells), F32),
            pltpu.VMEM(ocean_mask.shape, jnp.int32),
            pltpu.SMEM(flux_coef.shape, F32),
            pltpu.SemaphoreType.DMA((2 * fields + 2,)),
        ],
        10**7,
    )(field, edge, ver, *in_hbm(flux_coef, ocean_mask))
    received = gathered(received)
    return call(
        functools.partial(ocean_kernel, comps),
        jax.ShapeDtypeStruct(column_state.shape, F32),
        [HBM, VMEM, VMEM, VMEM],
        HBM,
        [pltpu.VMEM((fields, 1, cells), F32), pltpu.SemaphoreType.DMA((fields,))],
        10**6,
        aliases={0: 0},
    )(out, low, received, land)


def solution(mesh):
    placed = (
        P("comp", "tile", None, None, None),
        P(),
        P(),
        P(),
        P("comp", "tile", None),
        P("comp", "tile", None),
        P("comp", "tile", None),
        P("comp", "tile", None, None, None),
        P("tile", None),
    )
    return jax.shard_map(
        step,
        mesh=mesh,
        in_specs=placed,
        out_specs=P("comp", "tile", None, None, None),
        check_vma=False,
    )
```
